32 devices in a mesh: dp: 4 (over y, x), tile: 8 (over z, core).
Axes of the slice: x: 2, y: 2, z: 4, core: 2. Of those that a mesh axis runs over, the one named last changes fastest.
Arguments:
- features: bfloat16 [4, 8, 512, 1280], P('dp', 'tile'), may hold values from -6 to 6
- visible: int32 [4, 8, 512], P('dp', 'tile'), may hold values from 0 to 1, as said below
- positions: int32 [4, 8, 512], P('dp', 'tile'), may hold values from 0 to 511, each once within a row
- cotangent: bfloat16 [4, 8, 512, 512], P('dp', 'tile'), may hold values from -6 to 6
- mlp_gain: float32 [1280], replicated, may hold values from 0.1 to 1.9
- mlp_bias: float32 [1280], replicated, may hold values from -3 to 3
- fc1_weight: bfloat16 [1280, 2560], replicated, may hold values from -0.15625 to 0.15625
- fc1_bias: float32 [2560], replicated, may hold values from -3 to 3
- fc2_weight: bfloat16 [2560, 1280], replicated, may hold values from -0.125 to 0.125
- fc2_bias: float32 [1280], replicated, may hold values from -3 to 3
- encoder_gain: float32 [1280], replicated, may hold values from 0.1 to 1.9
- encoder_bias: float32 [1280], replicated, may hold values from -3 to 3
- embed_weight: bfloat16 [1280, 512], replicated, may hold values from -0.15625 to 0.15625
- embed_bias: float32 [512], replicated, may hold values from -3 to 3
- mask_token: float32 [512], replicated, may hold values from -4 to 4
- position_table: bfloat16 [512, 512], replicated, may hold values from -4 to 4
- decoder_gain: float32 [512], replicated, may hold values from 0.1 to 1.9
- decoder_bias: float32 [512], replicated, may hold values from -3 to 3
Outputs:
- feature_grad: bfloat16 [4, 8, 512, 1280], P('dp', 'tile')
- decoded: bfloat16 [4, 8, 512, 512], P('dp', 'tile')
- fc1_grad: float32 [1280, 2560], P('tile')
- fc2_grad: float32 [2560, 1280], P('tile')
The draws below stay inside these ranges and needn't reach their ends.
Inputs may be any that keep to these rules, and one draw needn't show every extreme that they name: In each scene (all 8 chips of one index of the first dimension) exactly 1024 patches are visible; each chip has at most 256 visible patches, and in every scene one chip has exactly 256. Each chip's position ids are a permutation of its 512 positions.
All inputs are finite; a program needn't handle non-finite values.
Results may differ from the reference program's by a relative error of at most 0.007.
Values may be sent and summed in bfloat16 or wider, within the bound.
A program may use at most 128 MiB of HBM per device.

```python
import jax
import jax.numpy as jnp
from jax import lax

D = 1280
DD = 512
HID = 2560
PATCHES = 512
SCENES = 4
TILES = 8
KEEP = 1024
MOST = 256
N_DP = 4
N_TILE = 8


def draw_visible(key, part):

    def one_scene(scene_key):
        key_busy, key_weight, key_perm = jax.random.split(scene_key, 3)
        tile_ids = jnp.arange(TILES, dtype=jnp.int32)
        busiest = jax.random.randint(key_busy, (), 0, TILES, dtype=jnp.int32)
        weights = jax.random.randint(key_weight, (TILES,), 2, 5, dtype=jnp.int32)
        weights = jnp.where(tile_ids == busiest, 0, weights)
        remain = KEEP - MOST
        portion = remain * weights // jnp.sum(weights)
        leftover = remain - jnp.sum(portion)
        others_rank = jnp.cumsum((weights > 0).astype(jnp.int32)) - 1
        portion = portion + ((weights > 0) & (others_rank < leftover)).astype(jnp.int32)
        chip_counts = jnp.where(tile_ids == busiest, MOST, portion)
        perm_keys = jax.random.split(key_perm, TILES)

        def one_chip(chip_key):
            return jax.random.permutation(chip_key, PATCHES).astype(jnp.int32)
        priority = jax.vmap(one_chip)(perm_keys)
        return (priority < chip_counts[:, None]).astype(jnp.int32)
    scene_keys = jax.random.split(key, SCENES)
    return jax.vmap(one_scene)(scene_keys)


def shard_levels(rng, shape, shards, low, high):
    factor_of, own = 1.0, jax.random.fold_in(rng, 6)
    for axis_at, parts in shards:
        steps = jnp.exp(jax.random.uniform(jax.random.fold_in(own, axis_at), (parts,), jnp.float32, low / len(shards), high / len(shards)))
        factor_of = factor_of * jnp.repeat(steps, shape[axis_at] // parts).reshape([-1 if axis == axis_at else 1 for axis in range(len(shape))])
    return factor_of


def noise(rng, extent, deviation, limit, cuts=(), held_as=jnp.bfloat16):
    drawn = jax.random.normal(rng, extent, jnp.float32) * deviation
    if len(cuts) > 0:
        drawn = shard_levels(rng, extent, cuts, -0.22, 0.18) * drawn
    return jnp.clip(drawn, min=-limit, max=limit).astype(held_as)


def setup_inputs(seed: int = 0) -> dict:
    seeds = jax.random.split(jax.random.key(seed), 19)
    features = noise(seeds[0], (SCENES, TILES, PATCHES, D), 1.0, 6.0, ((0, 4), (1, 8)))
    visible = draw_visible(jax.random.fold_in(seeds[18], 71), 0)
    positions = jax.vmap(lambda own: jax.random.permutation(own, PATCHES))(jax.random.split(seeds[2], SCENES * TILES)).reshape((SCENES, TILES, PATCHES)).astype(jnp.int32)
    cotangent = noise(seeds[3], (SCENES, TILES, PATCHES, DD), 1.0, 6.0, ((0, 4), (1, 8)))
    mlp_gain = jnp.clip(1.0 + 0.18 * jax.random.normal(seeds[4], (D,), jnp.float32), 0.1, 1.9)
    mlp_bias = noise(seeds[5], (D,), 0.5, 3.0, (), jnp.float32)
    fc1_weight = noise(seeds[6], (D, HID), D ** -0.5, 0.15625)
    fc1_bias = noise(seeds[7], (HID,), 0.5, 3.0, (), jnp.float32)
    fc2_weight = noise(seeds[8], (HID, D), HID ** -0.5, 0.125)
    fc2_bias = noise(seeds[9], (D,), 0.5, 3.0, (), jnp.float32)
    encoder_gain = jnp.clip(1.0 + 0.18 * jax.random.normal(seeds[10], (D,), jnp.float32), 0.1, 1.9)
    encoder_bias = noise(seeds[11], (D,), 0.5, 3.0, (), jnp.float32)
    embed_weight = noise(seeds[12], (D, DD), D ** -0.5, 0.15625)
    embed_bias = noise(seeds[13], (DD,), 0.5, 3.0, (), jnp.float32)
    mask_token = noise(seeds[14], (DD,), 1.0, 4.0, (), jnp.float32)
    position_table = noise(seeds[15], (PATCHES, DD), 0.7, 4.0)
    decoder_gain = jnp.clip(1.0 + 0.18 * jax.random.normal(seeds[16], (DD,), jnp.float32), 0.1, 1.9)
    decoder_bias = noise(seeds[17], (DD,), 0.5, 3.0, (), jnp.float32)
    return {"features": features, "visible": visible, "positions": positions, "cotangent": cotangent, "mlp_gain": mlp_gain, "mlp_bias": mlp_bias, "fc1_weight": fc1_weight, "fc1_bias": fc1_bias, "fc2_weight": fc2_weight, "fc2_bias": fc2_bias, "encoder_gain": encoder_gain, "encoder_bias": encoder_bias, "embed_weight": embed_weight, "embed_bias": embed_bias, "mask_token": mask_token, "position_table": position_table, "decoder_gain": decoder_gain, "decoder_bias": decoder_bias}


epsilon = 1e-06

def layer_norm(values, norm_gain, norm_bias):
    row_mean = lax.optimization_barrier(jnp.mean(values, axis=-1, keepdims=True))
    centred = values - row_mean
    variance = lax.optimization_barrier(jnp.mean(centred * centred, axis=-1, keepdims=True))
    inv_std = lax.rsqrt(variance + epsilon)
    scaled = centred * inv_std
    return (scaled * norm_gain + norm_bias, scaled, inv_std)

def norm_back(upstream, scaled, inv_std):
    mean_up = lax.optimization_barrier(jnp.mean(upstream, axis=-1, keepdims=True))
    mean_cross = lax.optimization_barrier(jnp.mean(upstream * scaled, axis=-1, keepdims=True))
    return inv_std * (upstream - mean_up - scaled * mean_cross)

def gelu_parts(pre_act):
    normal_cdf = 0.5 * (1.0 + lax.erf(pre_act * 0.7071067811865476))
    density = jnp.exp(-0.5 * pre_act * pre_act) * 0.3989422804014327
    return (pre_act * normal_cdf, normal_cdf + pre_act * density)

def reference(features, visible, positions, cotangent, mlp_gain, mlp_bias, fc1_weight, fc1_bias, fc2_weight, fc2_bias, encoder_gain, encoder_bias, embed_weight, embed_bias, mask_token, position_table, decoder_gain, decoder_bias):
    row_count = TILES * PATCHES

    def scene_step(carry, inputs):
        fc1_sum, fc2_sum = carry
        scene_feats, scene_vis, scene_pos, scene_cot = inputs
        row_data = scene_feats.reshape(-1, D)
        flags = scene_vis.reshape(-1).astype(jnp.int32)
        keep_rows = (flags > 0)[:, None]
        rank = jnp.cumsum(flags).astype(jnp.int32) - flags
        target = jnp.where(flags > 0, rank, row_count).astype(jnp.int32)
        order = jnp.zeros((row_count,), jnp.int32).at[target].set(jnp.arange(row_count, dtype=jnp.int32), mode='drop')
        compact = order[:KEEP]
        rows_in = jnp.take(row_data, compact, axis=0).astype(jnp.float32)
        mlp_in, mlp_scaled, mlp_inv = layer_norm(rows_in, mlp_gain, mlp_bias)
        mlp_in = mlp_in.astype(jnp.bfloat16)
        pre_act = jnp.dot(mlp_in, fc1_weight, preferred_element_type=jnp.float32) + fc1_bias
        activation, slope = gelu_parts(pre_act)
        hidden = activation.astype(jnp.bfloat16)
        encoded = rows_in + jnp.dot(hidden, fc2_weight, preferred_element_type=jnp.float32) + fc2_bias
        normed, enc_scaled, enc_inv = layer_norm(encoded, encoder_gain, encoder_bias)
        normed = normed.astype(jnp.bfloat16)
        projected = (jnp.dot(normed, embed_weight, preferred_element_type=jnp.float32) + embed_bias).astype(jnp.bfloat16)
        projected_full = jnp.zeros((row_count, DD), jnp.bfloat16).at[compact].set(projected)
        placed = jnp.take(position_table, scene_pos.reshape(-1), axis=0).astype(jnp.float32)
        dec_input = jnp.where(keep_rows, projected_full.astype(jnp.float32), mask_token) + placed
        decoded, dec_scaled, dec_inv = layer_norm(dec_input, decoder_gain, decoder_bias)
        upstream = scene_cot.reshape(-1, DD).astype(jnp.float32)
        grad_input = norm_back(upstream * decoder_gain, dec_scaled, dec_inv)
        grad_projected = jnp.where(keep_rows, grad_input, 0.0).astype(jnp.bfloat16)
        grad_compact = jnp.take(grad_projected, compact, axis=0)
        grad_normed = jnp.dot(grad_compact, embed_weight.T, preferred_element_type=jnp.float32)
        grad_encoded = norm_back(grad_normed * encoder_gain, enc_scaled, enc_inv).astype(jnp.bfloat16)
        grad_hidden = jnp.dot(grad_encoded, fc2_weight.T, preferred_element_type=jnp.float32)
        grad_pre = (grad_hidden * slope).astype(jnp.bfloat16)
        grad_mlp_in = jnp.dot(grad_pre, fc1_weight.T, preferred_element_type=jnp.float32)
        grad_feats = (grad_encoded.astype(jnp.float32) + norm_back(grad_mlp_in * mlp_gain, mlp_scaled, mlp_inv)).astype(jnp.bfloat16)
        fc1_term = jnp.dot(mlp_in.T, grad_pre, preferred_element_type=jnp.float32)
        fc2_term = jnp.dot(hidden.T, grad_encoded, preferred_element_type=jnp.float32)
        grad_rows = jnp.zeros((row_count, D), jnp.bfloat16).at[compact].set(grad_feats)
        outputs = (grad_rows.reshape(TILES, PATCHES, D), decoded.astype(jnp.bfloat16).reshape(TILES, PATCHES, DD))
        return ((fc1_sum + fc1_term, fc2_sum + fc2_term), outputs)
    start_carry = (jnp.zeros((D, HID), jnp.float32), jnp.zeros((HID, D), jnp.float32))
    final_carry, stacked = lax.scan(scene_step, start_carry, (features, visible, positions, cotangent))
    fc1_sum, fc2_sum = final_carry
    feature_grad, decoded = stacked
    device_total = N_DP * N_TILE
    return (feature_grad, decoded, fc1_sum / device_total, fc2_sum / device_total)
```

```python
import functools

import jax
import jax.numpy as jnp
from jax import lax
from jax.experimental import pallas as pl
from jax.experimental.pallas import tpu as pltpu
from jax.sharding import PartitionSpec as P

MESH = pl.DeviceIdType.MESH

epsilon = 1e-06


def layer_norm(values, norm_gain, norm_bias):
    row_mean = jnp.mean(values, axis=-1, keepdims=True)
    centred = values - row_mean
    variance = jnp.mean(centred * centred, axis=-1, keepdims=True)
    inv_std = lax.rsqrt(variance + epsilon)
    scaled = centred * inv_std
    return (scaled * norm_gain + norm_bias, scaled, inv_std)


def norm_back(upstream, scaled, inv_std):
    mean_up = jnp.mean(upstream, axis=-1, keepdims=True)
    mean_cross = jnp.mean(upstream * scaled, axis=-1, keepdims=True)
    return inv_std * (upstream - mean_up - scaled * mean_cross)


def gelu_parts(pre_act):
    normal_cdf = 0.5 * (1.0 + lax.erf(pre_act * 0.7071067811865476))
    density = jnp.exp(-0.5 * pre_act * pre_act) * 0.3989422804014327
    return (pre_act * normal_cdf, normal_cdf + pre_act * density)


def encode(enc_input, enc_params):
    (
        mlp_gain,
        mlp_bias,
        fc1_weight,
        fc1_bias,
        fc2_weight,
        fc2_bias,
        encoder_gain,
        encoder_bias,
        embed_weight,
        embed_bias,
    ) = enc_params
    rows_in = enc_input.astype(jnp.float32)
    mlp_in, mlp_scaled, mlp_inv = layer_norm(rows_in, mlp_gain, mlp_bias)
    mlp_in = mlp_in.astype(jnp.bfloat16)
    pre_act = jnp.dot(mlp_in, fc1_weight, preferred_element_type=jnp.float32) + fc1_bias
    activation, slope = gelu_parts(pre_act)
    hidden = activation.astype(jnp.bfloat16)
    encoded = rows_in + jnp.dot(hidden, fc2_weight, preferred_element_type=jnp.float32) + fc2_bias
    normed, enc_scaled, enc_inv = layer_norm(encoded, encoder_gain, encoder_bias)
    normed = normed.astype(jnp.bfloat16)
    projected = (
        jnp.dot(normed, embed_weight, preferred_element_type=jnp.float32) + embed_bias
    ).astype(jnp.bfloat16)
    saved = (mlp_in, mlp_scaled, mlp_inv, slope, hidden, enc_scaled, enc_inv)
    return (saved, projected)


def encode_back(saved, grad_compact, enc_params):
    (
        mlp_gain,
        mlp_bias,
        fc1_weight,
        fc1_bias,
        fc2_weight,
        fc2_bias,
        encoder_gain,
        encoder_bias,
        embed_weight,
        embed_bias,
    ) = enc_params
    mlp_in, mlp_scaled, mlp_inv, slope, hidden, enc_scaled, enc_inv = saved
    grad_normed = jnp.dot(grad_compact, embed_weight.T, preferred_element_type=jnp.float32)
    grad_encoded = norm_back(grad_normed * encoder_gain, enc_scaled, enc_inv).astype(jnp.bfloat16)
    grad_hidden = jnp.dot(grad_encoded, fc2_weight.T, preferred_element_type=jnp.float32)
    grad_pre = (grad_hidden * slope).astype(jnp.bfloat16)
    grad_mlp_in = jnp.dot(grad_pre, fc1_weight.T, preferred_element_type=jnp.float32)
    grad_feats = (
        grad_encoded.astype(jnp.float32) + norm_back(grad_mlp_in * mlp_gain, mlp_scaled, mlp_inv)
    ).astype(jnp.bfloat16)
    return (mlp_in, grad_pre, hidden, grad_encoded, grad_feats)


def decoder_pass(
    projected_rows,
    keep_rows,
    position_ids,
    upstream,
    position_table,
    mask_token,
    decoder_gain,
    decoder_bias,
):
    table_ids = jnp.arange(position_table.shape[0], dtype=jnp.int32)[None, :]
    pick = (position_ids[:, None] == table_ids).astype(jnp.bfloat16)
    placed = jnp.dot(pick, position_table, preferred_element_type=jnp.float32)
    dec_input = jnp.where(keep_rows, projected_rows, mask_token) + placed
    decoded, dec_scaled, dec_inv = layer_norm(dec_input, decoder_gain, decoder_bias)
    grad_input = norm_back(upstream.astype(jnp.float32) * decoder_gain, dec_scaled, dec_inv)
    grad_projected = jnp.where(keep_rows, grad_input, 0.0).astype(jnp.bfloat16)
    return (decoded.astype(jnp.bfloat16), grad_projected)


LANES = 128


def reduce_kernel(
    chunks,
    z_count,
    lhs_a,
    far_a,
    rhs_a,
    lhs_b,
    far_b,
    rhs_b,
    weight,
    gain,
    scaled,
    inverse,
    scatter,
    out_a,
    out_b,
    feature_out,
    weight_held,
    upstream,
    grad_rows,
    turned_a,
    turned_b,
    rhs_cat_a,
    rhs_cat_b,
    gathered_a,
    gathered_b,
    acc_a,
    acc_b,
    core_send_a,
    core_send_b,
    core_land_a,
    core_land_b,
    half_send_a,
    half_send_b,
    half_land_a,
    half_land_b,
    z_send_a,
    z_send_b,
    z_land_a,
    z_land_b,
    late_sems,
    pair_sems,
    z_sems,
    spread_sems,
    weight_sem,
):
    dp = lax.axis_index("dp")
    tile = lax.axis_index("tile")
    x = lax.rem(dp, 2)
    y = lax.div(dp, 2)
    core = lax.rem(tile, 2)
    my_z = lax.div(tile, 2)
    sibling = (dp, tile + 1 - 2 * core)
    across_x = (dp + 1 - 2 * x, tile)
    across_y = (dp + 2 - 4 * y, tile)
    diagonal = (3 - dp, tile)
    z_to = [lax.rem(my_z + k, z_count) for k in range(1, z_count)]
    peers = [sibling, across_x, across_y, diagonal]
    peers += [(dp, 2 * z + core) for z in z_to]

    fetch = pltpu.make_async_copy(weight, weight_held, weight_sem)
    fetch.start()
    barrier = pltpu.get_barrier_semaphore()
    for peer in peers:
        pl.semaphore_signal(barrier, inc=1, device_id=peer, device_id_type=MESH)
    pl.semaphore_wait(barrier, len(peers))

    batch = rhs_a.shape[0]
    block = turned_a.shape[1] // z_count
    half = chunks * LANES
    turned = (turned_a, turned_b)
    rhs = (rhs_a, rhs_b)
    rhs_cat = (rhs_cat_a, rhs_cat_b)
    gathered = (gathered_a, gathered_b)
    acc = (acc_a, acc_b)
    core_send, core_land = (core_send_a, core_send_b), (core_land_a, core_land_b)
    half_send, half_land = (half_send_a, half_send_b), (half_land_a, half_land_b)
    z_send, z_land = (z_send_a, z_send_b), (z_land_a, z_land_b)
    gather_peer = (across_x, across_y)
    half_peer = (across_y, across_x)
    kept = (y, x)
    own_base = (x * 2 * half, 0)
    far_base = ((1 - x) * 2 * half, 0)
    copies = {}

    def send(key, src, dst, sems, at, peer):
        copy = pltpu.make_async_remote_copy(
            src_ref=src,
            dst_ref=dst,
            send_sem=sems.at[(0,) + at],
            recv_sem=sems.at[(1,) + at],
            device_id=peer,
            device_id_type=MESH,
        )
        copy.start()
        copies[key] = copy

    def late(t, j):
        for h in range(2):
            first = pl.multiple_of(far_base[t] + h * half + j * LANES, LANES)
            send(
                ("l", t, j, h),
                rhs[t].at[:, pl.ds(first, LANES)],
                rhs_cat[t].at[j, batch : 2 * batch, h * LANES : (h + 1) * LANES],
                late_sems,
                (t, j, h),
                gather_peer[t],
            )

    def turn():
        for side, source in enumerate((lhs_a, far_a)):
            for at in range(0, source.shape[1], 256):
                flipped = source[:, at : at + 256].T
                row = at
                while row < at + 256:
                    number = row // block
                    stop = min(at + 256, (number + 1) * block)
                    first = (number // 2) * block + row - number * block
                    turned_a[
                        number % 2,
                        first : first + stop - row,
                        side * batch : (side + 1) * batch,
                    ] = flipped[row - at : stop - at]
                    row = stop
        for side, source in enumerate((lhs_b, far_b)):
            for c in range(2):
                turned_b[c, :, side * batch : (side + 1) * batch] = source[c]

    def products(t, j, which, store):
        @pl.loop(0, z_count // 2)
        def _(pair):
            first = pl.multiple_of(pair * 2 * block, 16)
            part = jnp.dot(
                turned[t][which, pl.ds(first, 2 * block), :],
                rhs_cat[t][j],
                preferred_element_type=jnp.float32,
            )
            for e in range(2):
                for h in range(2):
                    store(
                        h,
                        2 * pair + e,
                        part[e * block : (e + 1) * block, h * LANES : (h + 1) * LANES],
                    )

    def stage0(t, j):
        def store_send(h, z, value):
            core_send[t][j, h, z] = value.astype(jnp.bfloat16)

        def store_own(h, z, value):
            acc[t][j, h, z] = value

        for h in range(2):
            first = pl.multiple_of(own_base[t] + h * half + j * LANES, LANES)
            rhs_cat[t][j, 0:batch, h * LANES : (h + 1) * LANES] = rhs[t][:, pl.ds(first, LANES)]
        for h in range(2):
            copies["l", t, j, h].wait()
        products(t, j, 1 - core, store_send)
        send(("c", t, j), core_send[t].at[j], core_land[t].at[j], pair_sems, (0, t, j), sibling)
        products(t, j, core, store_own)

    def stage1(t, j):
        r = kept[t]
        copies["c", t, j].wait()

        @pl.loop(0, z_count)
        def _(z):
            half_send[t][j, z] = (
                acc[t][j, 1 - r, z] + core_land[t][j, 1 - r, z].astype(jnp.float32)
            ).astype(jnp.bfloat16)

        send(
            ("h", t, j), half_send[t].at[j], half_land[t].at[j], pair_sems, (1, t, j), half_peer[t]
        )

        @pl.loop(0, z_count)
        def _(z):
            acc[t][j, r, z] = acc[t][j, r, z] + core_land[t][j, r, z].astype(jnp.float32)

    def stage2(t, j):
        r = kept[t]
        copies["h", t, j].wait()
        for k, z in enumerate(z_to):
            z_send[t][j, k] = (
                acc[t][j, r, z] + half_land[t][j, z].astype(jnp.float32)
            ).astype(jnp.bfloat16)
            send(
                ("z", t, j, k),
                z_send[t].at[j, k],
                z_land[t].at[j, k],
                z_sems,
                (t, j, k),
                (dp, 2 * z + core),
            )
        acc[t][j, r, my_z] = acc[t][j, r, my_z] + half_land[t][j, my_z].astype(jnp.float32)

    def stage3(t, j):
        total = acc[t][j, kept[t], my_z]
        for k in range(z_count - 1):
            copies["z", t, j, k].wait()
            total = total + z_land[t][j, k].astype(jnp.float32)
        mine = 2 * x + y
        gathered[t][mine, j] = total.astype(jnp.bfloat16)
        for k, peer in enumerate((across_x, across_y, diagonal)):
            send(
                ("s", t, j, k),
                gathered[t].at[mine, j],
                gathered[t].at[mine, j],
                spread_sems,
                (t, j, k),
                peer,
            )

    def stage4(t, j):
        for k in range(3):
            copies["s", t, j, k].wait()
        for mine in range(4):
            if t == 0:
                first = mine * half + j * LANES
                out_a[:, first : first + LANES] = gathered[t][mine, j]
            else:
                row, first = (mine % 2) * block, (mine // 2) * half + j * LANES
                out_b[row : row + block, first : first + LANES] = gathered[t][mine, j]

    def feature_columns(q):
        if q == 0:
            fetch.wait()
        wide = weight_held.shape[0] // chunks
        at = slice(q * wide, (q + 1) * wide)
        part = lax.dot_general(
            rhs_a[...],
            weight_held[at, :],
            (((1,), (1,)), ((), ())),
            preferred_element_type=jnp.float32,
        )
        upstream[:, at] = part * gain[:, at]

    def feature_rows():
        tall = upstream.shape[0] // 8

        @pl.loop(0, 8)
        def _(i):
            at = pl.ds(pl.multiple_of(i * tall, tall), tall)
            back = norm_back(upstream[at, :], scaled[at, :], inverse[at, :])
            grad_rows[at, :] = (rhs_b[at, :].astype(jnp.float32) + back).astype(jnp.bfloat16)

        wide = feature_out.shape[0] // 4

        @pl.loop(0, 4)
        def _(i):
            at = pl.ds(pl.multiple_of(i * wide, wide), wide)
            feature_out[at, :] = jnp.dot(
                scatter[at, :], grad_rows[...], preferred_element_type=jnp.float32
            ).astype(jnp.bfloat16)

    items = [(t, j) for j in range(chunks) for t in (1, 0)]
    stages = (stage0, stage1, stage2, stage3, stage4)
    ahead = 3
    for item in items[:ahead]:
        late(*item)
    turn()
    for step in range(len(items) + len(stages) - 1):
        if step + ahead < len(items):
            late(*items[step + ahead])
        for at in (1, 2, 3, 0, 4):
            i = step - at
            if 0 <= i < len(items):
                stages[at](*items[i])
        if 1 <= step <= chunks:
            feature_columns(step - 1)
        if step == chunks + 1:
            feature_rows()


def reduce_weights(
    mlp_in,
    mlp_far,
    grad_pre,
    hidden_turned,
    hidden_far,
    grad_encoded,
    tiles,
    fc1_weight,
    mlp_gain,
    mlp_scaled,
    mlp_inv,
    scatter,
):
    rows, width = mlp_in.shape
    inner = grad_pre.shape[1]
    z_count = tiles // 2
    block = width // tiles
    chunks = width // 2 // LANES
    whole = pl.BlockSpec(memory_space=pltpu.VMEM)
    half, full = jnp.bfloat16, jnp.float32
    scratch = [
        pltpu.VMEM((width, inner), half),
        pltpu.VMEM((rows, width), full),
        pltpu.VMEM((rows, width), half),
    ]
    for lead, kind in (
        ((2, z_count * block, 2 * rows), half),
        ((chunks, 2 * rows, 2 * LANES), half),
        ((4, chunks, block, LANES), half),
        ((chunks, 2, z_count, block, LANES), full),
        ((chunks, 2, z_count, block, LANES), half),
        ((chunks, 2, z_count, block, LANES), half),
        ((chunks, z_count, block, LANES), half),
        ((chunks, z_count, block, LANES), half),
        ((chunks, z_count - 1, block, LANES), half),
        ((chunks, z_count - 1, block, LANES), half),
    ):
        scratch += [pltpu.VMEM(lead, kind)] * 2
    scratch += [
        pltpu.SemaphoreType.DMA((2, 2, chunks, 2)),
        pltpu.SemaphoreType.DMA((2, 2, 2, chunks)),
        pltpu.SemaphoreType.DMA((2, 2, chunks, z_count - 1)),
        pltpu.SemaphoreType.DMA((2, 2, chunks, 3)),
        pltpu.SemaphoreType.DMA,
    ]
    out_a, out_b, features = pl.pallas_call(
        functools.partial(reduce_kernel, chunks, z_count),
        out_shape=(
            jax.ShapeDtypeStruct((block, inner), half),
            jax.ShapeDtypeStruct((2 * block, width), half),
            jax.ShapeDtypeStruct((scatter.shape[0], width), half),
        ),
        in_specs=[whole] * 6 + [pl.BlockSpec(memory_space=pl.ANY)] + [whole] * 4,
        out_specs=(whole, whole, whole),
        scratch_shapes=scratch,
        compiler_params=pltpu.CompilerParams(
            collective_id=0, has_side_effects=True, vmem_limit_bytes=56 * 2**20
        ),
    )(
        mlp_in,
        mlp_far,
        grad_pre,
        hidden_turned,
        hidden_far,
        grad_encoded,
        fc1_weight,
        mlp_gain[None, :],
        mlp_scaled,
        mlp_inv,
        scatter,
    )
    return (out_a.astype(full), out_b.astype(full)), features


def reducible(width, inner, scenes, tiles):
    return (
        scenes == 4
        and tiles % 4 == 0
        and inner == 2 * width
        and width % (tiles * 16) == 0
        and width % 256 == 0
    )


def shards(
    features,
    visible,
    positions,
    cotangent,
    mlp_gain,
    mlp_bias,
    fc1_weight,
    fc1_bias,
    fc2_weight,
    fc2_bias,
    encoder_gain,
    encoder_bias,
    embed_weight,
    embed_bias,
    mask_token,
    position_table,
    decoder_gain,
    decoder_bias,
):
    patch_count = features.shape[2]
    model_width = features.shape[3]
    dec_width = embed_weight.shape[1]
    most_rows = patch_count // 2
    flags = visible.reshape(patch_count)
    row_data = features.reshape(patch_count, model_width)
    keep_rows = (flags > 0)[:, None]
    upstream = cotangent.reshape(patch_count, dec_width)
    ids = jnp.arange(patch_count, dtype=jnp.int32)
    row_rank = jnp.sum(jnp.where(ids[None, :] < ids[:, None], flags[None, :], 0), axis=1)
    slots = jnp.arange(most_rows, dtype=jnp.int32)
    target = jnp.where(flags > 0, row_rank, -1)
    gather = (slots[:, None] == target[None, :]).astype(jnp.bfloat16)
    scatter = (target[:, None] == slots[None, :]).astype(jnp.bfloat16)
    enc_params = (
        mlp_gain,
        mlp_bias,
        fc1_weight,
        fc1_bias,
        fc2_weight,
        fc2_bias,
        encoder_gain,
        encoder_bias,
        embed_weight,
        embed_bias,
    )
    decoder_args = (position_table, mask_token, decoder_gain, decoder_bias)
    enc_input = jnp.dot(gather, row_data, preferred_element_type=jnp.bfloat16)
    saved, projected = encode(enc_input, enc_params)
    projected_rows = jnp.dot(scatter, projected, preferred_element_type=jnp.float32)
    decoded, grad_projected = decoder_pass(
        projected_rows, keep_rows, positions.reshape(-1), upstream, *decoder_args
    )
    grad_compact = jnp.dot(gather, grad_projected, preferred_element_type=jnp.bfloat16)
    device_total = lax.axis_size("dp") * lax.axis_size("tile")
    tiles = lax.axis_size("tile")
    inner = fc1_weight.shape[1]
    small = reducible(model_width, inner, lax.axis_size("dp"), tiles)
    if small:
        mlp_far = lax.ppermute(saved[0], "dp", [(d, d ^ 1) for d in range(4)])
        dp = lax.axis_index("dp")
        split = saved[4].T.reshape(tiles // 2, 2, 2, inner // tiles // 2, most_rows)

        def y_half(which):
            part = lax.dynamic_index_in_dim(split, which, 2, keepdims=False)
            return part.transpose(1, 0, 2, 3).reshape(2, -1, most_rows)

        hidden_turned = y_half(dp // 2)
        hidden_far = lax.ppermute(
            y_half(1 - dp // 2), "dp", [(d, d ^ 2) for d in range(4)]
        )
    mlp_in, grad_pre, hidden, grad_encoded, grad_feats = encode_back(
        saved, grad_compact, enc_params
    )
    if small:
        totals, grad_rows = reduce_weights(
            mlp_in,
            mlp_far,
            grad_pre,
            hidden_turned,
            hidden_far,
            grad_encoded,
            tiles,
            fc1_weight,
            mlp_gain,
            saved[1],
            saved[2],
            scatter,
        )
    else:
        grad_rows = jnp.dot(scatter, grad_feats, preferred_element_type=jnp.bfloat16)
        totals = []
        for left, right in ((mlp_in, grad_pre), (hidden, grad_encoded)):
            term = jnp.dot(left.T, right, preferred_element_type=jnp.float32)
            share = lax.psum_scatter(
                term.astype(jnp.bfloat16), "tile", scatter_dimension=0, tiled=True
            )
            totals.append(lax.psum(share, "dp").astype(jnp.float32))
    fc1_grad, fc2_grad = [total / device_total for total in totals]
    feature_grad = grad_rows.reshape(features.shape)
    decoded_out = decoded.reshape(cotangent.shape)
    return (feature_grad, decoded_out, fc1_grad, fc2_grad)


def solution(mesh):
    return jax.shard_map(
        shards,
        mesh=mesh,
        in_specs=(
            P("dp", "tile", None, None),
            P("dp", "tile", None),
            P("dp", "tile", None),
            P("dp", "tile", None, None),
            P(),
            P(),
            P(),
            P(),
            P(),
            P(),
            P(),
            P(),
            P(),
            P(),
            P(),
            P(),
            P(),
            P(),
        ),
        out_specs=(
            P("dp", "tile", None, None),
            P("dp", "tile", None, None),
            P("tile", None),
            P("tile", None),
        ),
        check_vma=False,
    )
```

```python
import functools

import jax
import jax.numpy as jnp
from jax import lax
from jax.experimental import pallas as pl
from jax.experimental.pallas import tpu as pltpu
from jax.sharding import PartitionSpec as P

MESH = pl.DeviceIdType.MESH

epsilon = 1e-06


def layer_norm(values, norm_gain, norm_bias):
    row_mean = jnp.mean(values, axis=-1, keepdims=True)
    centred = values - row_mean
    variance = jnp.mean(centred * centred, axis=-1, keepdims=True)
    inv_std = lax.rsqrt(variance + epsilon)
    scaled = centred * inv_std
    return (scaled * norm_gain + norm_bias, scaled, inv_std)


def norm_back(upstream, scaled, inv_std):
    mean_up = jnp.mean(upstream, axis=-1, keepdims=True)
    mean_cross = jnp.mean(upstream * scaled, axis=-1, keepdims=True)
    return inv_std * (upstream - mean_up - scaled * mean_cross)


def gelu_parts(pre_act):
    normal_cdf = 0.5 * (1.0 + lax.erf(pre_act * 0.7071067811865476))
    density = jnp.exp(-0.5 * pre_act * pre_act) * 0.3989422804014327
    return (pre_act * normal_cdf, normal_cdf + pre_act * density)


def encode(enc_input, enc_params):
    (
        mlp_gain,
        mlp_bias,
        fc1_weight,
        fc1_bias,
        fc2_weight,
        fc2_bias,
        encoder_gain,
        encoder_bias,
        embed_weight,
        embed_bias,
    ) = enc_params
    rows_in = enc_input.astype(jnp.float32)
    mlp_in, mlp_scaled, mlp_inv = layer_norm(rows_in, mlp_gain, mlp_bias)
    mlp_in = mlp_in.astype(jnp.bfloat16)
    pre_act = jnp.dot(mlp_in, fc1_weight, preferred_element_type=jnp.float32) + fc1_bias
    activation, slope = gelu_parts(pre_act)
    hidden = activation.astype(jnp.bfloat16)
    encoded = rows_in + jnp.dot(hidden, fc2_weight, preferred_element_type=jnp.float32) + fc2_bias
    normed, enc_scaled, enc_inv = layer_norm(encoded, encoder_gain, encoder_bias)
    normed = normed.astype(jnp.bfloat16)
    projected = (
        jnp.dot(normed, embed_weight, preferred_element_type=jnp.float32) + embed_bias
    ).astype(jnp.bfloat16)
    saved = (mlp_in, mlp_scaled, mlp_inv, slope, hidden, enc_scaled, enc_inv)
    return (saved, projected)


def encode_back(saved, grad_compact, enc_params):
    (
        mlp_gain,
        mlp_bias,
        fc1_weight,
        fc1_bias,
        fc2_weight,
        fc2_bias,
        encoder_gain,
        encoder_bias,
        embed_weight,
        embed_bias,
    ) = enc_params
    mlp_in, mlp_scaled, mlp_inv, slope, hidden, enc_scaled, enc_inv = saved
    grad_normed = jnp.dot(grad_compact, embed_weight.T, preferred_element_type=jnp.float32)
    grad_encoded = norm_back(grad_normed * encoder_gain, enc_scaled, enc_inv).astype(jnp.bfloat16)
    grad_hidden = jnp.dot(grad_encoded, fc2_weight.T, preferred_element_type=jnp.float32)
    grad_pre = (grad_hidden * slope).astype(jnp.bfloat16)
    grad_mlp_in = jnp.dot(grad_pre, fc1_weight.T, preferred_element_type=jnp.float32)
    grad_feats = (
        grad_encoded.astype(jnp.float32) + norm_back(grad_mlp_in * mlp_gain, mlp_scaled, mlp_inv)
    ).astype(jnp.bfloat16)
    return (mlp_in, grad_pre, hidden, grad_encoded, grad_feats)


def decoder_pass(
    projected_rows,
    keep_rows,
    position_ids,
    upstream,
    position_table,
    mask_token,
    decoder_gain,
    decoder_bias,
):
    table_ids = jnp.arange(position_table.shape[0], dtype=jnp.int32)[None, :]
    pick = (position_ids[:, None] == table_ids).astype(jnp.bfloat16)
    placed = jnp.dot(pick, position_table, preferred_element_type=jnp.float32)
    dec_input = jnp.where(keep_rows, projected_rows, mask_token) + placed
    decoded, dec_scaled, dec_inv = layer_norm(dec_input, decoder_gain, decoder_bias)
    grad_input = norm_back(upstream.astype(jnp.float32) * decoder_gain, dec_scaled, dec_inv)
    grad_projected = jnp.where(keep_rows, grad_input, 0.0).astype(jnp.bfloat16)
    return (decoded.astype(jnp.bfloat16), grad_projected)


LANES = 128
WIDE = 256


def normalize(values):
    row_mean = jnp.mean(values, axis=-1, keepdims=True)
    centred = values - row_mean
    variance = jnp.mean(centred * centred, axis=-1, keepdims=True)
    inv_std = lax.rsqrt(variance + epsilon)
    return (centred * inv_std, inv_std)


def nt_dot(left, right):
    return lax.dot_general(
        left, right, (((1,), (1,)), ((), ())), preferred_element_type=jnp.float32
    )


def nn_dot(left, right):
    return jnp.dot(left, right, preferred_element_type=jnp.float32)


def fused_kernel(
    chunks,
    z_count,
    visible,
    positions,
    mlp_gain,
    mlp_bias,
    fc1_bias,
    fc2_bias,
    encoder_gain,
    encoder_bias,
    embed_bias,
    mask_token,
    decoder_gain,
    decoder_bias,
    features,
    cotangent,
    fc1_weight,
    fc2_weight,
    embed_weight,
    position_table,
    out_a,
    out_b,
    feature_out,
    decoded_out,
    feats,
    cot,
    fc1,
    fc2,
    embed,
    table,
    gather,
    scatter,
    rows_in,
    mlp_scaled,
    mlp_inv,
    mlp_in,
    hidden,
    slope,
    by_half,
    encoded,
    enc_inv,
    normed,
    projected,
    placed,
    placed_rows,
    cot_rows,
    grad_rows,
    upstream,
    grad_encoded,
    grad_pre,
    turned_a,
    turned_b,
    rhs_cat_a,
    rhs_cat_b,
    gathered_a,
    gathered_b,
    acc_a,
    acc_b,
    core_send_a,
    core_send_b,
    core_land_a,
    core_land_b,
    half_send_a,
    half_send_b,
    half_land_a,
    half_land_b,
    z_send_a,
    z_send_b,
    z_land_a,
    z_land_b,
    load_sems,
    early_sems,
    late_sems,
    pair_sems,
    z_sems,
    spread_sems,
):
    half_type, full_type = jnp.bfloat16, jnp.float32
    dp = lax.axis_index("dp")
    tile = lax.axis_index("tile")
    x = lax.rem(dp, 2)
    y = lax.div(dp, 2)
    core = lax.rem(tile, 2)
    my_z = lax.div(tile, 2)
    sibling = (dp, tile + 1 - 2 * core)
    across_x = (dp + 1 - 2 * x, tile)
    across_y = (dp + 2 - 4 * y, tile)
    diagonal = (3 - dp, tile)
    z_to = [lax.rem(my_z + k, z_count) for k in range(1, z_count)]
    peers = [sibling, across_x, across_y, diagonal]
    peers += [(dp, 2 * z + core) for z in z_to]

    barrier = pltpu.get_barrier_semaphore()
    for peer in peers:
        pl.semaphore_signal(barrier, inc=1, device_id=peer, device_id_type=MESH)
    loads = []
    for k, (source, held) in enumerate(
        (
            (features, feats),
            (fc1_weight, fc1),
            (fc2_weight, fc2),
            (position_table, table),
            (cotangent, cot),
            (embed_weight, embed),
        )
    ):
        load = pltpu.make_async_copy(source, held, load_sems.at[k])
        load.start()
        loads.append(load)
    load_feats, load_fc1, load_fc2, load_table, load_cot, load_embed = loads

    patches, width = feats.shape
    batch, inner = hidden.shape
    block = turned_a.shape[1] // z_count
    half = chunks * LANES
    turned = (turned_a, turned_b)
    rhs = (grad_pre, grad_encoded)
    rhs_cat = (rhs_cat_a, rhs_cat_b)
    gathered = (gathered_a, gathered_b)
    acc = (acc_a, acc_b)
    core_send, core_land = (core_send_a, core_send_b), (core_land_a, core_land_b)
    half_send, half_land = (half_send_a, half_send_b), (half_land_a, half_land_b)
    z_send, z_land = (z_send_a, z_send_b), (z_land_a, z_land_b)
    gather_peer = (across_x, across_y)
    half_peer = (across_y, across_x)
    kept = (y, x)
    own_base = (x * 2 * half, 0)
    far_base = ((1 - x) * 2 * half, 0)
    copies = {}

    def send(key, src, dst, sems, at, peer):
        copy = pltpu.make_async_remote_copy(
            src_ref=src,
            dst_ref=dst,
            send_sem=sems.at[(0,) + at],
            recv_sem=sems.at[(1,) + at],
            device_id=peer,
            device_id_type=MESH,
        )
        copy.start()
        copies[key] = copy

    def row_blocks(count, tall, body):
        @pl.loop(0, count)
        def _(i):
            body(pl.ds(pl.multiple_of(i * tall, tall), tall))

    def column_blocks(count, body):
        @pl.loop(0, count)
        def _(i):
            body(pl.ds(pl.multiple_of(i * WIDE, WIDE), WIDE))

    flags = visible[...] > 0
    ones = jnp.broadcast_to(jnp.where(flags, 1.0, 0.0), (16, patches)).astype(half_type)
    before = lax.broadcasted_iota(jnp.int32, (patches, patches), 0) < lax.broadcasted_iota(
        jnp.int32, (patches, patches), 1
    )
    rank = nn_dot(ones, jnp.where(before, 1.0, 0.0).astype(half_type))[0:1, :]
    target = jnp.where(flags, rank, -1.0).astype(jnp.int32)
    slot = lax.broadcasted_iota(jnp.int32, (batch, patches), 0)
    gather[...] = jnp.where(slot == target, 1.0, 0.0).astype(half_type)
    load_feats.wait()

    def compact(at):
        rows_in[:, at] = nn_dot(gather[...], feats[:, at]).astype(half_type)

    column_blocks(width // WIDE, compact)

    def first_norm(at):
        scaled, inverse = normalize(rows_in[at, :].astype(full_type))
        mlp_scaled[at, :] = scaled
        mlp_inv[at, :] = inverse
        mlp_in[at, :] = (scaled * mlp_gain[...] + mlp_bias[...]).astype(half_type)

    row_blocks(batch // 32, 32, first_norm)
    for at in range(0, width, WIDE):
        flipped = mlp_in[:, at : at + WIDE].T
        row = at
        while row < at + WIDE:
            number = row // block
            stop = min(at + WIDE, (number + 1) * block)
            first = (number // 2) * block + row - number * block
            turned_a[number % 2, first : first + stop - row, 0:batch] = flipped[
                row - at : stop - at
            ]
            row = stop
    pl.semaphore_wait(barrier, len(peers))
    send(
        ("e", 0, 0),
        turned_a.at[:, :, 0:batch],
        turned_a.at[:, :, batch : 2 * batch],
        early_sems,
        (0, 0),
        across_x,
    )

    load_fc1.wait()
    group = 8 * block
    for i in range(inner // group):
        for at in range(0, group, WIDE):
            columns = slice(i * group + at, i * group + at + WIDE)
            pre_act = nn_dot(mlp_in[...], fc1[:, columns]) + fc1_bias[:, columns]
            activation, slope[:, columns] = gelu_parts(pre_act)
            activation = activation.astype(half_type)
            hidden[:, columns] = activation
            flipped = activation.T
            row = at
            while row < at + WIDE:
                number = row // block
                stop = min(at + WIDE, (number + 1) * block)
                first = (2 * i + number // 4) * block + row - number * block
                by_half[
                    number % 2, (number // 2) % 2, first : first + stop - row, :
                ] = flipped[row - at : stop - at]
                row = stop
        part = slice(2 * i * block, 2 * (i + 1) * block)
        send(
            ("e", 1, i),
            by_half.at[1 - y, :, part, :],
            turned_b.at[:, part, batch : 2 * batch],
            early_sems,
            (1, i),
            across_y,
        )
    turned_b[:, :, 0:batch] = by_half[y]

    load_fc2.wait()

    def second_product(at):
        encoded[:, at] = (
            rows_in[:, at].astype(full_type) + nn_dot(hidden[...], fc2[:, at]) + fc2_bias[:, at]
        )

    column_blocks(width // WIDE, second_product)

    def second_norm(at):
        scaled, inverse = normalize(encoded[at, :])
        encoded[at, :] = scaled
        enc_inv[at, :] = inverse
        normed[at, :] = (scaled * encoder_gain[...] + encoder_bias[...]).astype(half_type)

    row_blocks(batch // 32, 32, second_norm)
    load_table.wait()
    load_cot.wait()
    names = lax.broadcasted_iota(jnp.int32, (patches, patches), 0)
    pick = jnp.where(names == positions[...], 1.0, 0.0).astype(half_type).T
    placed[...] = nn_dot(pick, table[...]).astype(half_type)
    placed_rows[...] = nn_dot(gather[...], placed[...]).astype(half_type)
    cot_rows[...] = nn_dot(gather[...], cot[...]).astype(half_type)
    load_embed.wait()
    projected[...] = (nn_dot(normed[...], embed[...]) + embed_bias[...]).astype(half_type)

    def decoder_rows(at):
        scaled, inverse = normalize(
            projected[at, :].astype(full_type) + placed_rows[at, :].astype(full_type)
        )
        back = norm_back(cot_rows[at, :].astype(full_type) * decoder_gain[...], scaled, inverse)
        grad_rows[at, :] = back.astype(half_type)

    row_blocks(batch // 32, 32, decoder_rows)

    def embed_back(at):
        upstream[:, at] = nt_dot(grad_rows[...], embed[at, :]) * encoder_gain[:, at]

    column_blocks(width // WIDE, embed_back)

    def encoder_back(at):
        grad_encoded[at, :] = norm_back(upstream[at, :], encoded[at, :], enc_inv[at, :]).astype(
            half_type
        )

    row_blocks(batch // 32, 32, encoder_back)

    def late(t, j):
        for h in range(2):
            first = pl.multiple_of(far_base[t] + h * half + j * LANES, LANES)
            send(
                ("l", t, j, h),
                rhs[t].at[:, pl.ds(first, LANES)],
                rhs_cat[t].at[j, batch : 2 * batch, h * LANES : (h + 1) * LANES],
                late_sems,
                (t, j, h),
                gather_peer[t],
            )

    def pre_columns(base, j, own):
        at = [
            pl.ds(pl.multiple_of(base + h * half + j * LANES, LANES), LANES) for h in range(2)
        ]
        weights = jnp.concatenate([fc2[at[0], :], fc2[at[1], :]], axis=0)
        part = nt_dot(grad_encoded[...], weights)
        for h in range(2):
            value = (part[:, h * LANES : (h + 1) * LANES] * slope[:, at[h]]).astype(half_type)
            grad_pre[:, at[h]] = value
            if own:
                rhs_cat_a[j, 0:batch, h * LANES : (h + 1) * LANES] = value

    ahead = 2
    for j in range(ahead):
        late(1, j)
    for j in range(chunks):
        pre_columns(far_base[0], j, False)
        if j < ahead:
            late(0, j)
    for j in range(chunks):
        pre_columns(own_base[0], j, True)

    def feature_columns(at):
        upstream[:, at] = nt_dot(grad_pre[...], fc1[at, :]) * mlp_gain[:, at]

    def feature_rows(at):
        back = norm_back(upstream[at, :], mlp_scaled[at, :], mlp_inv[at, :])
        normed[at, :] = (grad_encoded[at, :].astype(full_type) + back).astype(half_type)

    def feature_place(at):
        feats[at, :] = nn_dot(scatter[at, :], normed[...]).astype(half_type)

    def decoder_place(at):
        picks = scatter[at, :]
        keep_rows = jnp.sum(picks.astype(full_type), axis=1, keepdims=True) > 0.5
        rows = jnp.where(keep_rows, nn_dot(picks, projected[...]), mask_token[...])
        scaled, _ = normalize(rows + placed[at, :].astype(full_type))
        cot[at, :] = (scaled * decoder_gain[...] + decoder_bias[...]).astype(half_type)

    stores = []

    def store(k, source, target):
        copy = pltpu.make_async_copy(source, target, load_sems.at[k])
        copy.start()
        stores.append(copy)

    def feature_part(k):
        if k == 0:
            scatter[...] = gather[...].T
            row_blocks(patches // 64, 64, decoder_place)
            store(0, cot, decoded_out)
        if k == 1:
            column_blocks(width // WIDE, feature_columns)
        if k == 2:
            row_blocks(batch // 32, 32, feature_rows)
            row_blocks(patches // 128, 128, feature_place)
            store(1, feats, feature_out)

    def products(t, j, which, put):
        @pl.loop(0, z_count // 2)
        def _(pair):
            first = pl.multiple_of(pair * 2 * block, 16)
            part = nn_dot(turned[t][which, pl.ds(first, 2 * block), :], rhs_cat[t][j])
            for e in range(2):
                for h in range(2):
                    put(
                        h,
                        2 * pair + e,
                        part[e * block : (e + 1) * block, h * LANES : (h + 1) * LANES],
                    )

    def stage0(t, j):
        def put_send(h, z, value):
            core_send[t][j % 2, h, z] = value.astype(half_type)

        def put_own(h, z, value):
            acc[t][j, h, z] = value

        if j == 0:
            for i in range(1 if t == 0 else inner // group):
                copies["e", t, i].wait()
        if t == 1:
            for h in range(2):
                first = pl.multiple_of(h * half + j * LANES, LANES)
                rhs_cat_b[j, 0:batch, h * LANES : (h + 1) * LANES] = grad_encoded[
                    :, pl.ds(first, LANES)
                ]
        for h in range(2):
            copies["l", t, j, h].wait()
        products(t, j, 1 - core, put_send)
        send(
            ("c", t, j), core_send[t].at[j % 2], core_land[t].at[j], pair_sems, (0, t, j), sibling
        )
        products(t, j, core, put_own)

    def stage1(t, j):
        r = kept[t]
        copies["c", t, j].wait()

        @pl.loop(0, z_count)
        def _(z):
            half_send[t][j % 2, z] = (
                acc[t][j, 1 - r, z] + core_land[t][j, 1 - r, z].astype(full_type)
            ).astype(half_type)

        send(
            ("h", t, j),
            half_send[t].at[j % 2],
            half_land[t].at[j],
            pair_sems,
            (1, t, j),
            half_peer[t],
        )

        @pl.loop(0, z_count)
        def _(z):
            acc[t][j, r, z] = acc[t][j, r, z] + core_land[t][j, r, z].astype(full_type)

    def stage2(t, j):
        r = kept[t]
        copies["h", t, j].wait()
        for k, z in enumerate(z_to):
            z_send[t][j % 2, k] = (
                acc[t][j, r, z] + half_land[t][j, z].astype(full_type)
            ).astype(half_type)
            send(
                ("z", t, j, k),
                z_send[t].at[j % 2, k],
                z_land[t].at[j, k],
                z_sems,
                (t, j, k),
                (dp, 2 * z + core),
            )
        acc[t][j, r, my_z] = acc[t][j, r, my_z] + half_land[t][j, my_z].astype(full_type)

    def stage3(t, j):
        total = acc[t][j, kept[t], my_z]
        for k in range(z_count - 1):
            copies["z", t, j, k].wait()
            total = total + z_land[t][j, k].astype(full_type)
        mine = 2 * x + y
        gathered[t][mine, j] = total.astype(half_type)
        for k, peer in enumerate((across_x, across_y, diagonal)):
            send(
                ("s", t, j, k),
                gathered[t].at[mine, j],
                gathered[t].at[mine, j],
                spread_sems,
                (t, j, k),
                peer,
            )

    def stage4(t, j):
        for k in range(3):
            copies["s", t, j, k].wait()
        for mine in range(4):
            if t == 0:
                first = mine * half + j * LANES
                out_a[:, first : first + LANES] = gathered[t][mine, j]
            else:
                row, first = (mine % 2) * block, (mine // 2) * half + j * LANES
                out_b[row : row + block, first : first + LANES] = gathered[t][mine, j]

    feature_part(0)
    feature_part(1)
    items = [(t, j) for j in range(chunks) for t in (0, 1)]
    stages = ((stage1, 2), (stage2, 4), (stage3, 6), (stage0, 0), (stage4, 8))
    for step in range(len(items) + 8):
        if step + 2 * ahead < len(items):
            late(*items[step + 2 * ahead])
        for stage, lag in stages:
            i = step - lag
            if 0 <= i < len(items):
                stage(*items[i])
        if step == 1:
            feature_part(2)
    for copy in stores:
        copy.wait()


def fused(row_data, upstream_rows, visible, positions, matrices, vectors, tiles):
    patches, width = row_data.shape
    fc1_weight, fc2_weight, embed_weight, position_table = matrices
    inner, dec_width = fc1_weight.shape[1], embed_weight.shape[1]
    rows = patches // 2
    z_count = tiles // 2
    block = width // tiles
    chunks = width // 2 // LANES
    whole = pl.BlockSpec(memory_space=pltpu.VMEM)
    away = pl.BlockSpec(memory_space=pl.ANY)
    half, full = jnp.bfloat16, jnp.float32
    shapes = [
        ((patches, width), half),
        ((patches, dec_width), half),
        (fc1_weight.shape, half),
        (fc2_weight.shape, half),
        (embed_weight.shape, half),
        (position_table.shape, half),
        ((rows, patches), half),
        ((patches, rows), half),
        ((rows, width), half),
        ((rows, width), full),
        ((rows, 1), full),
        ((rows, width), half),
        ((rows, inner), half),
        ((rows, inner), full),
        ((2, 2, z_count * block, rows), half),
        ((rows, width), full),
        ((rows, 1), full),
        ((rows, width), half),
        ((rows, dec_width), half),
        ((patches, dec_width), half),
        ((rows, dec_width), half),
        ((rows, dec_width), half),
        ((rows, dec_width), half),
        ((rows, width), full),
        ((rows, width), half),
        ((rows, inner), half),
    ]
    for lead, kind in (
        ((2, z_count * block, 2 * rows), half),
        ((chunks, 2 * rows, 2 * LANES), half),
        ((4, chunks, block, LANES), half),
        ((chunks, 2, z_count, block, LANES), full),
        ((2, 2, z_count, block, LANES), half),
        ((chunks, 2, z_count, block, LANES), half),
        ((2, z_count, block, LANES), half),
        ((chunks, z_count, block, LANES), half),
        ((2, z_count - 1, block, LANES), half),
        ((chunks, z_count - 1, block, LANES), half),
    ):
        shapes += [(lead, kind)] * 2
    scratch = [pltpu.VMEM(lead, kind) for lead, kind in shapes]
    scratch += [
        pltpu.SemaphoreType.DMA((6,)),
        pltpu.SemaphoreType.DMA((2, 2, 2)),
        pltpu.SemaphoreType.DMA((2, 2, chunks, 2)),
        pltpu.SemaphoreType.DMA((2, 2, 2, chunks)),
        pltpu.SemaphoreType.DMA((2, 2, chunks, z_count - 1)),
        pltpu.SemaphoreType.DMA((2, 2, chunks, 3)),
    ]
    return pl.pallas_call(
        functools.partial(fused_kernel, chunks, z_count),
        out_shape=(
            jax.ShapeDtypeStruct((block, inner), half),
            jax.ShapeDtypeStruct((2 * block, width), half),
            jax.ShapeDtypeStruct((patches, width), half),
            jax.ShapeDtypeStruct((patches, dec_width), half),
        ),
        in_specs=[whole] * 12 + [away] * 6,
        out_specs=(whole, whole, away, away),
        scratch_shapes=scratch,
        compiler_params=pltpu.CompilerParams(
            collective_id=0, has_side_effects=True, vmem_limit_bytes=60 * 2**20
        ),
    )(
        visible.reshape(1, patches),
        positions.reshape(1, patches),
        *[vector.reshape(1, -1) for vector in vectors],
        row_data,
        upstream_rows,
        fc1_weight,
        fc2_weight,
        embed_weight,
        position_table,
    )


def reducible(patches, width, inner, dec_width, scenes, tiles):
    return (
        scenes == 4
        and tiles == 8
        and inner == 2 * width
        and width % (tiles * 16) == 0
        and width % WIDE == 0
        and (width // tiles * 8) % WIDE == 0
        and inner % (width // tiles * 8) == 0
        and inner // (width // tiles * 8) == 2
        and patches % 256 == 0
        and dec_width % LANES == 0
    )


def shards(
    features,
    visible,
    positions,
    cotangent,
    mlp_gain,
    mlp_bias,
    fc1_weight,
    fc1_bias,
    fc2_weight,
    fc2_bias,
    encoder_gain,
    encoder_bias,
    embed_weight,
    embed_bias,
    mask_token,
    position_table,
    decoder_gain,
    decoder_bias,
):
    patch_count = features.shape[2]
    model_width = features.shape[3]
    dec_width = embed_weight.shape[1]
    tiles = lax.axis_size("tile")
    scenes = lax.axis_size("dp")
    most_rows = patch_count // 2
    flags = visible.reshape(patch_count)
    row_data = features.reshape(patch_count, model_width)
    if reducible(
        patch_count, model_width, fc1_weight.shape[1], dec_width, scenes, tiles
    ):
        total_a, total_b, grad_rows, decoded = fused(
            row_data,
            cotangent.reshape(patch_count, dec_width),
            visible,
            positions,
            (fc1_weight, fc2_weight, embed_weight, position_table),
            (
                mlp_gain,
                mlp_bias,
                fc1_bias,
                fc2_bias,
                encoder_gain,
                encoder_bias,
                embed_bias,
                mask_token,
                decoder_gain,
                decoder_bias,
            ),
            tiles,
        )
        device_total = scenes * tiles
        return (
            grad_rows.reshape(features.shape),
            decoded.reshape(cotangent.shape),
            total_a.astype(jnp.float32) / device_total,
            total_b.astype(jnp.float32) / device_total,
        )
    keep_rows = (flags > 0)[:, None]
    upstream = cotangent.reshape(patch_count, dec_width)
    ids = jnp.arange(patch_count, dtype=jnp.int32)
    row_rank = jnp.sum(jnp.where(ids[None, :] < ids[:, None], flags[None, :], 0), axis=1)
    slots = jnp.arange(most_rows, dtype=jnp.int32)
    target = jnp.where(flags > 0, row_rank, -1)
    gather = (slots[:, None] == target[None, :]).astype(jnp.bfloat16)
    scatter = (target[:, None] == slots[None, :]).astype(jnp.bfloat16)
    enc_params = (
        mlp_gain,
        mlp_bias,
        fc1_weight,
        fc1_bias,
        fc2_weight,
        fc2_bias,
        encoder_gain,
        encoder_bias,
        embed_weight,
        embed_bias,
    )
    decoder_args = (position_table, mask_token, decoder_gain, decoder_bias)
    enc_input = jnp.dot(gather, row_data, preferred_element_type=jnp.bfloat16)
    saved, projected = encode(enc_input, enc_params)
    projected_rows = jnp.dot(scatter, projected, preferred_element_type=jnp.float32)
    decoded, grad_projected = decoder_pass(
        projected_rows, keep_rows, positions.reshape(-1), upstream, *decoder_args
    )
    grad_compact = jnp.dot(gather, grad_projected, preferred_element_type=jnp.bfloat16)
    mlp_in, grad_pre, hidden, grad_encoded, grad_feats = encode_back(
        saved, grad_compact, enc_params
    )
    device_total = scenes * tiles
    grad_rows = jnp.dot(scatter, grad_feats, preferred_element_type=jnp.bfloat16)
    totals = []
    for left, right in ((mlp_in, grad_pre), (hidden, grad_encoded)):
        term = jnp.dot(left.T, right, preferred_element_type=jnp.float32)
        share = lax.psum_scatter(
            term.astype(jnp.bfloat16), "tile", scatter_dimension=0, tiled=True
        )
        totals.append(lax.psum(share, "dp").astype(jnp.float32))
    fc1_grad, fc2_grad = [total / device_total for total in totals]
    feature_grad = grad_rows.reshape(features.shape)
    decoded_out = decoded.reshape(cotangent.shape)
    return (feature_grad, decoded_out, fc1_grad, fc2_grad)


def solution(mesh):
    return jax.shard_map(
        shards,
        mesh=mesh,
        in_specs=(
            P("dp", "tile", None, None),
            P("dp", "tile", None),
            P("dp", "tile", None),
            P("dp", "tile", None, None),
            P(),
            P(),
            P(),
            P(),
            P(),
            P(),
            P(),
            P(),
            P(),
            P(),
            P(),
            P(),
            P(),
            P(),
        ),
        out_specs=(
            P("dp", "tile", None, None),
            P("dp", "tile", None, None),
            P("tile", None),
            P("tile", None),
        ),
        check_vma=False,
    )
```

```python
import functools

import jax
import jax.numpy as jnp
from jax import lax
from jax.experimental import pallas as pl
from jax.experimental.pallas import tpu as pltpu
from jax.sharding import PartitionSpec as P

MESH = pl.DeviceIdType.MESH

epsilon = 1e-06


def layer_norm(values, norm_gain, norm_bias):
    row_mean = jnp.mean(values, axis=-1, keepdims=True)
    centred = values - row_mean
    variance = jnp.mean(centred * centred, axis=-1, keepdims=True)
    inv_std = lax.rsqrt(variance + epsilon)
    scaled = centred * inv_std
    return (scaled * norm_gain + norm_bias, scaled, inv_std)


def norm_back(upstream, scaled, inv_std):
    mean_up = jnp.mean(upstream, axis=-1, keepdims=True)
    mean_cross = jnp.mean(upstream * scaled, axis=-1, keepdims=True)
    return inv_std * (upstream - mean_up - scaled * mean_cross)


def gelu_parts(pre_act):
    normal_cdf = 0.5 * (1.0 + lax.erf(pre_act * 0.7071067811865476))
    density = jnp.exp(-0.5 * pre_act * pre_act) * 0.3989422804014327
    return (pre_act * normal_cdf, normal_cdf + pre_act * density)


def encode(enc_input, enc_params):
    (
        mlp_gain,
        mlp_bias,
        fc1_weight,
        fc1_bias,
        fc2_weight,
        fc2_bias,
        encoder_gain,
        encoder_bias,
        embed_weight,
        embed_bias,
    ) = enc_params
    rows_in = enc_input.astype(jnp.float32)
    mlp_in, mlp_scaled, mlp_inv = layer_norm(rows_in, mlp_gain, mlp_bias)
    mlp_in = mlp_in.astype(jnp.bfloat16)
    pre_act = jnp.dot(mlp_in, fc1_weight, preferred_element_type=jnp.float32) + fc1_bias
    activation, slope = gelu_parts(pre_act)
    hidden = activation.astype(jnp.bfloat16)
    encoded = rows_in + jnp.dot(hidden, fc2_weight, preferred_element_type=jnp.float32) + fc2_bias
    normed, enc_scaled, enc_inv = layer_norm(encoded, encoder_gain, encoder_bias)
    normed = normed.astype(jnp.bfloat16)
    projected = (
        jnp.dot(normed, embed_weight, preferred_element_type=jnp.float32) + embed_bias
    ).astype(jnp.bfloat16)
    saved = (mlp_in, mlp_scaled, mlp_inv, slope, hidden, enc_scaled, enc_inv)
    return (saved, projected)


def encode_back(saved, grad_compact, enc_params):
    (
        mlp_gain,
        mlp_bias,
        fc1_weight,
        fc1_bias,
        fc2_weight,
        fc2_bias,
        encoder_gain,
        encoder_bias,
        embed_weight,
        embed_bias,
    ) = enc_params
    mlp_in, mlp_scaled, mlp_inv, slope, hidden, enc_scaled, enc_inv = saved
    grad_normed = jnp.dot(grad_compact, embed_weight.T, preferred_element_type=jnp.float32)
    grad_encoded = norm_back(grad_normed * encoder_gain, enc_scaled, enc_inv).astype(jnp.bfloat16)
    grad_hidden = jnp.dot(grad_encoded, fc2_weight.T, preferred_element_type=jnp.float32)
    grad_pre = (grad_hidden * slope).astype(jnp.bfloat16)
    grad_mlp_in = jnp.dot(grad_pre, fc1_weight.T, preferred_element_type=jnp.float32)
    grad_feats = (
        grad_encoded.astype(jnp.float32) + norm_back(grad_mlp_in * mlp_gain, mlp_scaled, mlp_inv)
    ).astype(jnp.bfloat16)
    return (mlp_in, grad_pre, hidden, grad_encoded, grad_feats)


def decoder_pass(
    projected_rows,
    keep_rows,
    position_ids,
    upstream,
    position_table,
    mask_token,
    decoder_gain,
    decoder_bias,
):
    table_ids = jnp.arange(position_table.shape[0], dtype=jnp.int32)[None, :]
    pick = (position_ids[:, None] == table_ids).astype(jnp.bfloat16)
    placed = jnp.dot(pick, position_table, preferred_element_type=jnp.float32)
    dec_input = jnp.where(keep_rows, projected_rows, mask_token) + placed
    decoded, dec_scaled, dec_inv = layer_norm(dec_input, decoder_gain, decoder_bias)
    grad_input = norm_back(upstream.astype(jnp.float32) * decoder_gain, dec_scaled, dec_inv)
    grad_projected = jnp.where(keep_rows, grad_input, 0.0).astype(jnp.bfloat16)
    return (decoded.astype(jnp.bfloat16), grad_projected)


LANES = 128
WIDE = 256


def normalize(values):
    row_mean = jnp.mean(values, axis=-1, keepdims=True)
    centred = values - row_mean
    variance = jnp.mean(centred * centred, axis=-1, keepdims=True)
    inv_std = lax.rsqrt(variance + epsilon)
    return (centred * inv_std, inv_std)


def nt_dot(left, right):
    return lax.dot_general(
        left, right, (((1,), (1,)), ((), ())), preferred_element_type=jnp.float32
    )


def nn_dot(left, right):
    return jnp.dot(left, right, preferred_element_type=jnp.float32)


def fused_kernel(
    chunks,
    z_count,
    visible,
    positions,
    mlp_gain,
    mlp_bias,
    fc1_bias,
    fc2_bias,
    encoder_gain,
    encoder_bias,
    embed_bias,
    mask_token,
    decoder_gain,
    decoder_bias,
    features,
    cotangent,
    fc1_weight,
    fc2_weight,
    embed_weight,
    position_table,
    out_a,
    out_b,
    feature_out,
    decoded_out,
    vectors,
    feats,
    cot,
    fc1,
    fc2,
    embed,
    table,
    gather,
    scatter,
    rows_in,
    mlp_scaled,
    mlp_inv,
    mlp_in,
    hidden,
    slope,
    by_half,
    encoded,
    enc_inv,
    normed,
    projected,
    placed,
    placed_rows,
    cot_rows,
    grad_rows,
    upstream,
    grad_encoded,
    grad_pre,
    turned_a,
    turned_b,
    rhs_cat_a,
    rhs_cat_b,
    gathered_a,
    gathered_b,
    acc_a,
    acc_b,
    core_send_a,
    core_send_b,
    core_land_a,
    core_land_b,
    half_send_a,
    half_send_b,
    half_land_a,
    half_land_b,
    z_send_a,
    z_send_b,
    z_land_a,
    z_land_b,
    load_sems,
    early_sems,
    late_sems,
    pair_sems,
    z_sems,
    spread_sems,
):
    half_type, full_type = jnp.bfloat16, jnp.float32
    for row, vector in enumerate(
        (
            mlp_gain,
            mlp_bias,
            fc1_bias,
            fc2_bias,
            encoder_gain,
            encoder_bias,
            embed_bias,
            mask_token,
            decoder_gain,
            decoder_bias,
        )
    ):
        vectors[row : row + 1, 0 : vector.shape[0]] = vector[...].reshape(1, -1)
    (
        mlp_gain,
        mlp_bias,
        fc1_bias,
        fc2_bias,
        encoder_gain,
        encoder_bias,
        embed_bias,
        mask_token,
        decoder_gain,
        decoder_bias,
    ) = [
        vectors.at[row : row + 1, 0 : vector.shape[0]]
        for row, vector in enumerate(
            (
                mlp_gain,
                mlp_bias,
                fc1_bias,
                fc2_bias,
                encoder_gain,
                encoder_bias,
                embed_bias,
                mask_token,
                decoder_gain,
                decoder_bias,
            )
        )
    ]
    dp = lax.axis_index("dp")
    tile = lax.axis_index("tile")
    x = lax.rem(dp, 2)
    y = lax.div(dp, 2)
    core = lax.rem(tile, 2)
    my_z = lax.div(tile, 2)
    sibling = (dp, tile + 1 - 2 * core)
    across_x = (dp + 1 - 2 * x, tile)
    across_y = (dp + 2 - 4 * y, tile)
    diagonal = (3 - dp, tile)
    z_to = [lax.rem(my_z + k, z_count) for k in range(1, z_count)]
    peers = [sibling, across_x, across_y, diagonal]
    peers += [(dp, 2 * z + core) for z in z_to]

    barrier = pltpu.get_barrier_semaphore()
    for peer in peers:
        pl.semaphore_signal(barrier, inc=1, device_id=peer, device_id_type=MESH)
    loads = []
    for k, (source, held) in enumerate(
        (
            (features, feats),
            (fc1_weight, fc1),
            (fc2_weight, fc2),
            (position_table, table),
            (cotangent, cot),
            (embed_weight, embed),
        )
    ):
        load = pltpu.make_async_copy(source, held, load_sems.at[k])
        load.start()
        loads.append(load)
    load_feats, load_fc1, load_fc2, load_table, load_cot, load_embed = loads

    patches, width = feats.shape
    batch, inner = hidden.shape
    block = turned_a.shape[1] // z_count
    half = chunks * LANES
    turned = (turned_a, turned_b)
    rhs = (grad_pre, grad_encoded)
    rhs_cat = (rhs_cat_a, rhs_cat_b)
    gathered = (gathered_a, gathered_b)
    acc = (acc_a, acc_b)
    core_send, core_land = (core_send_a, core_send_b), (core_land_a, core_land_b)
    half_send, half_land = (half_send_a, half_send_b), (half_land_a, half_land_b)
    z_send, z_land = (z_send_a, z_send_b), (z_land_a, z_land_b)
    gather_peer = (across_x, across_y)
    half_peer = (across_y, across_x)
    kept = (y, x)
    own_base = (x * 2 * half, 0)
    far_base = ((1 - x) * 2 * half, 0)
    copies = {}

    def send(key, src, dst, sems, at, peer):
        copy = pltpu.make_async_remote_copy(
            src_ref=src,
            dst_ref=dst,
            send_sem=sems.at[(0,) + at],
            recv_sem=sems.at[(1,) + at],
            device_id=peer,
            device_id_type=MESH,
        )
        copy.start()
        copies[key] = copy

    def row_blocks(count, tall, body):
        @pl.loop(0, count)
        def _(i):
            body(pl.ds(pl.multiple_of(i * tall, tall), tall))

    def column_blocks(count, body):
        @pl.loop(0, count)
        def _(i):
            body(pl.ds(pl.multiple_of(i * WIDE, WIDE), WIDE))

    flags = visible[...] > 0
    ones = jnp.broadcast_to(jnp.where(flags, 1.0, 0.0), (16, patches)).astype(half_type)
    before = lax.broadcasted_iota(jnp.int32, (patches, patches), 0) < lax.broadcasted_iota(
        jnp.int32, (patches, patches), 1
    )
    rank = nn_dot(ones, jnp.where(before, 1.0, 0.0).astype(half_type))[0:1, :]
    target = jnp.where(flags, rank, -1.0).astype(jnp.int32)
    slot = lax.broadcasted_iota(jnp.int32, (batch, patches), 0)
    gather[...] = jnp.where(slot == target, 1.0, 0.0).astype(half_type)
    load_feats.wait()

    def compact(at):
        rows_in[:, at] = nn_dot(gather[...], feats[:, at]).astype(half_type)

    column_blocks(width // WIDE, compact)

    def first_norm(at):
        scaled, inverse = normalize(rows_in[at, :].astype(full_type))
        mlp_scaled[at, :] = scaled
        mlp_inv[at, :] = inverse
        mlp_in[at, :] = (scaled * mlp_gain[...] + mlp_bias[...]).astype(half_type)

    row_blocks(batch // 32, 32, first_norm)
    for at in range(0, width, WIDE):
        flipped = mlp_in[:, at : at + WIDE].T
        row = at
        while row < at + WIDE:
            number = row // block
            stop = min(at + WIDE, (number + 1) * block)
            first = (number // 2) * block + row - number * block
            turned_a[number % 2, first : first + stop - row, 0:batch] = flipped[
                row - at : stop - at
            ]
            row = stop
    pl.semaphore_wait(barrier, len(peers))
    send(
        ("e", 0, 0),
        turned_a.at[:, :, 0:batch],
        turned_a.at[:, :, batch : 2 * batch],
        early_sems,
        (0, 0),
        across_x,
    )

    load_fc1.wait()
    group = 8 * block
    for i in range(inner // group):
        for at in range(0, group, WIDE):
            columns = slice(i * group + at, i * group + at + WIDE)
            pre_act = nn_dot(mlp_in[...], fc1[:, columns]) + fc1_bias[:, columns]
            activation, slope[:, columns] = gelu_parts(pre_act)
            activation = activation.astype(half_type)
            hidden[:, columns] = activation
            flipped = activation.T
            row = at
            while row < at + WIDE:
                number = row // block
                stop = min(at + WIDE, (number + 1) * block)
                first = (2 * i + number // 4) * block + row - number * block
                by_half[
                    number % 2, (number // 2) % 2, first : first + stop - row, :
                ] = flipped[row - at : stop - at]
                row = stop
        part = slice(2 * i * block, 2 * (i + 1) * block)
        send(
            ("e", 1, i),
            by_half.at[1 - y, :, part, :],
            turned_b.at[:, part, batch : 2 * batch],
            early_sems,
            (1, i),
            across_y,
        )
    turned_b[:, :, 0:batch] = by_half[y]

    load_fc2.wait()

    def second_product(at):
        encoded[:, at] = (
            rows_in[:, at].astype(full_type) + nn_dot(hidden[...], fc2[:, at]) + fc2_bias[:, at]
        )

    column_blocks(width // WIDE, second_product)

    def second_norm(at):
        scaled, inverse = normalize(encoded[at, :])
        encoded[at, :] = scaled
        enc_inv[at, :] = inverse
        normed[at, :] = (scaled * encoder_gain[...] + encoder_bias[...]).astype(half_type)

    row_blocks(batch // 32, 32, second_norm)
    load_table.wait()
    load_cot.wait()
    names = lax.broadcasted_iota(jnp.int32, (patches, patches), 0)
    pick = jnp.where(names == positions[...], 1.0, 0.0).astype(half_type).T
    placed[...] = nn_dot(pick, table[...]).astype(half_type)
    placed_rows[...] = nn_dot(gather[...], placed[...]).astype(half_type)
    cot_rows[...] = nn_dot(gather[...], cot[...]).astype(half_type)
    load_embed.wait()
    projected[...] = (nn_dot(normed[...], embed[...]) + embed_bias[...]).astype(half_type)

    def decoder_rows(at):
        scaled, inverse = normalize(
            projected[at, :].astype(full_type) + placed_rows[at, :].astype(full_type)
        )
        back = norm_back(cot_rows[at, :].astype(full_type) * decoder_gain[...], scaled, inverse)
        grad_rows[at, :] = back.astype(half_type)

    row_blocks(batch // 32, 32, decoder_rows)

    def embed_back(at):
        upstream[:, at] = nt_dot(grad_rows[...], embed[at, :]) * encoder_gain[:, at]

    column_blocks(width // WIDE, embed_back)

    def encoder_back(at):
        grad_encoded[at, :] = norm_back(upstream[at, :], encoded[at, :], enc_inv[at, :]).astype(
            half_type
        )

    row_blocks(batch // 32, 32, encoder_back)

    def late(t, j):
        for h in range(2):
            first = pl.multiple_of(far_base[t] + h * half + j * LANES, LANES)
            send(
                ("l", t, j, h),
                rhs[t].at[:, pl.ds(first, LANES)],
                rhs_cat[t].at[j, batch : 2 * batch, h * LANES : (h + 1) * LANES],
                late_sems,
                (t, j, h),
                gather_peer[t],
            )

    def pre_columns(base, j, own):
        at = [
            pl.ds(pl.multiple_of(base + h * half + j * LANES, LANES), LANES) for h in range(2)
        ]
        weights = jnp.concatenate([fc2[at[0], :], fc2[at[1], :]], axis=0)
        part = nt_dot(grad_encoded[...], weights)
        for h in range(2):
            value = (part[:, h * LANES : (h + 1) * LANES] * slope[:, at[h]]).astype(half_type)
            grad_pre[:, at[h]] = value
            if own:
                rhs_cat_a[j, 0:batch, h * LANES : (h + 1) * LANES] = value

    ahead = 2
    for j in range(ahead):
        late(1, j)
    for j in range(chunks):
        pre_columns(far_base[0], j, False)
        if j < ahead:
            late(0, j)
    for j in range(chunks):
        pre_columns(own_base[0], j, True)

    def feature_columns(at):
        upstream[:, at] = nt_dot(grad_pre[...], fc1[at, :]) * mlp_gain[:, at]

    def feature_rows(at):
        back = norm_back(upstream[at, :], mlp_scaled[at, :], mlp_inv[at, :])
        normed[at, :] = (grad_encoded[at, :].astype(full_type) + back).astype(half_type)

    def feature_place(at):
        feats[at, :] = nn_dot(scatter[at, :], normed[...]).astype(half_type)

    def decoder_place(at):
        picks = scatter[at, :]
        keep_rows = jnp.sum(picks.astype(full_type), axis=1, keepdims=True) > 0.5
        rows = jnp.where(keep_rows, nn_dot(picks, projected[...]), mask_token[...])
        scaled, _ = normalize(rows + placed[at, :].astype(full_type))
        cot[at, :] = (scaled * decoder_gain[...] + decoder_bias[...]).astype(half_type)

    stores = []

    def store(k, source, target):
        copy = pltpu.make_async_copy(source, target, load_sems.at[k])
        copy.start()
        stores.append(copy)

    def feature_part(k):
        if k == 0:
            scatter[...] = gather[...].T
            row_blocks(patches // 64, 64, decoder_place)
            store(0, cot, decoded_out)
        if k == 1:
            column_blocks(width // WIDE, feature_columns)
        if k == 2:
            row_blocks(batch // 32, 32, feature_rows)
            row_blocks(patches // 128, 128, feature_place)
            store(1, feats, feature_out)

    def products(t, j, which, put):
        @pl.loop(0, z_count // 2)
        def _(pair):
            first = pl.multiple_of(pair * 2 * block, 16)
            part = nn_dot(turned[t][which, pl.ds(first, 2 * block), :], rhs_cat[t][j])
            for e in range(2):
                for h in range(2):
                    put(
                        h,
                        2 * pair + e,
                        part[e * block : (e + 1) * block, h * LANES : (h + 1) * LANES],
                    )

    def stage0(t, j):
        def put_send(h, z, value):
            core_send[t][j % 2, h, z] = value.astype(half_type)

        def put_own(h, z, value):
            acc[t][j, h, z] = value

        if j == 0:
            for i in range(1 if t == 0 else inner // group):
                copies["e", t, i].wait()
        if t == 1:
            for h in range(2):
                first = pl.multiple_of(h * half + j * LANES, LANES)
                rhs_cat_b[j, 0:batch, h * LANES : (h + 1) * LANES] = grad_encoded[
                    :, pl.ds(first, LANES)
                ]
        for h in range(2):
            copies["l", t, j, h].wait()
        products(t, j, 1 - core, put_send)
        send(
            ("c", t, j), core_send[t].at[j % 2], core_land[t].at[j], pair_sems, (0, t, j), sibling
        )
        products(t, j, core, put_own)

    def stage1(t, j):
        r = kept[t]
        copies["c", t, j].wait()

        @pl.loop(0, z_count)
        def _(z):
            half_send[t][j % 2, z] = (
                acc[t][j, 1 - r, z] + core_land[t][j, 1 - r, z].astype(full_type)
            ).astype(half_type)

        send(
            ("h", t, j),
            half_send[t].at[j % 2],
            half_land[t].at[j],
            pair_sems,
            (1, t, j),
            half_peer[t],
        )

        @pl.loop(0, z_count)
        def _(z):
            acc[t][j, r, z] = acc[t][j, r, z] + core_land[t][j, r, z].astype(full_type)

    def stage2(t, j):
        r = kept[t]
        copies["h", t, j].wait()
        for k, z in enumerate(z_to):
            z_send[t][j % 2, k] = (
                acc[t][j, r, z] + half_land[t][j, z].astype(full_type)
            ).astype(half_type)
            send(
                ("z", t, j, k),
                z_send[t].at[j % 2, k],
                z_land[t].at[j, k],
                z_sems,
                (t, j, k),
                (dp, 2 * z + core),
            )
        acc[t][j, r, my_z] = acc[t][j, r, my_z] + half_land[t][j, my_z].astype(full_type)

    def stage3(t, j):
        total = acc[t][j, kept[t], my_z]
        for k in range(z_count - 1):
            copies["z", t, j, k].wait()
            total = total + z_land[t][j, k].astype(full_type)
        mine = 2 * x + y
        gathered[t][mine, j] = total.astype(half_type)
        for k, peer in enumerate((across_x, across_y, diagonal)):
            send(
                ("s", t, j, k),
                gathered[t].at[mine, j],
                gathered[t].at[mine, j],
                spread_sems,
                (t, j, k),
                peer,
            )

    def stage4(t, j):
        for k in range(3):
            copies["s", t, j, k].wait()
        for mine in range(4):
            if t == 0:
                first = mine * half + j * LANES
                out_a[:, first : first + LANES] = gathered[t][mine, j]
            else:
                row, first = (mine % 2) * block, (mine // 2) * half + j * LANES
                out_b[row : row + block, first : first + LANES] = gathered[t][mine, j]

    feature_part(0)
    feature_part(1)
    items = [(t, j) for j in range(chunks) for t in (0, 1)]
    stages = ((stage1, 2), (stage2, 4), (stage3, 6), (stage0, 0), (stage4, 8))
    for step in range(len(items) + 8):
        if step + 2 * ahead < len(items):
            late(*items[step + 2 * ahead])
        for stage, lag in stages:
            i = step - lag
            if 0 <= i < len(items):
                stage(*items[i])
        if step == 1:
            feature_part(2)
    for copy in stores:
        copy.wait()


def fused(row_data, upstream_rows, visible, positions, matrices, vectors, tiles):
    patches, width = row_data.shape
    fc1_weight, fc2_weight, embed_weight, position_table = matrices
    inner, dec_width = fc1_weight.shape[1], embed_weight.shape[1]
    rows = patches // 2
    z_count = tiles // 2
    block = width // tiles
    chunks = width // 2 // LANES
    whole = pl.BlockSpec(memory_space=pltpu.VMEM)
    away = pl.BlockSpec(memory_space=pl.ANY)
    half, full = jnp.bfloat16, jnp.float32
    shapes = [
        ((16, inner), full),
        ((patches, width), half),
        ((patches, dec_width), half),
        (fc1_weight.shape, half),
        (fc2_weight.shape, half),
        (embed_weight.shape, half),
        (position_table.shape, half),
        ((rows, patches), half),
        ((patches, rows), half),
        ((rows, width), half),
        ((rows, width), full),
        ((rows, 1), full),
        ((rows, width), half),
        ((rows, inner), half),
        ((rows, inner), full),
        ((2, 2, z_count * block, rows), half),
        ((rows, width), full),
        ((rows, 1), full),
        ((rows, width), half),
        ((rows, dec_width), half),
        ((patches, dec_width), half),
        ((rows, dec_width), half),
        ((rows, dec_width), half),
        ((rows, dec_width), half),
        ((rows, width), full),
        ((rows, width), half),
        ((rows, inner), half),
    ]
    for lead, kind in (
        ((2, z_count * block, 2 * rows), half),
        ((chunks, 2 * rows, 2 * LANES), half),
        ((4, chunks, block, LANES), half),
        ((chunks, 2, z_count, block, LANES), full),
        ((2, 2, z_count, block, LANES), half),
        ((chunks, 2, z_count, block, LANES), half),
        ((2, z_count, block, LANES), half),
        ((chunks, z_count, block, LANES), half),
        ((2, z_count - 1, block, LANES), half),
        ((chunks, z_count - 1, block, LANES), half),
    ):
        shapes += [(lead, kind)] * 2
    scratch = [pltpu.VMEM(lead, kind) for lead, kind in shapes]
    scratch += [
        pltpu.SemaphoreType.DMA((6,)),
        pltpu.SemaphoreType.DMA((2, 2, 2)),
        pltpu.SemaphoreType.DMA((2, 2, chunks, 2)),
        pltpu.SemaphoreType.DMA((2, 2, 2, chunks)),
        pltpu.SemaphoreType.DMA((2, 2, chunks, z_count - 1)),
        pltpu.SemaphoreType.DMA((2, 2, chunks, 3)),
    ]
    return pl.pallas_call(
        functools.partial(fused_kernel, chunks, z_count),
        out_shape=(
            jax.ShapeDtypeStruct((block, inner), half),
            jax.ShapeDtypeStruct((2 * block, width), half),
            jax.ShapeDtypeStruct((patches, width), half),
            jax.ShapeDtypeStruct((patches, dec_width), half),
        ),
        in_specs=[whole] * 12 + [away] * 6,
        out_specs=(whole, whole, away, away),
        scratch_shapes=scratch,
        compiler_params=pltpu.CompilerParams(
            collective_id=0, has_side_effects=True, vmem_limit_bytes=60 * 2**20
        ),
    )(
        visible.reshape(1, patches),
        positions.reshape(1, patches),
        *vectors,
        row_data,
        upstream_rows,
        fc1_weight,
        fc2_weight,
        embed_weight,
        position_table,
    )


def finish_kernel(
    steps, count, part_a, part_b, features, decoded, full_a, full_b, feature_out, decoded_out, sems
):
    moves = [
        pltpu.make_async_copy(features, feature_out, sems.at[0]),
        pltpu.make_async_copy(decoded, decoded_out, sems.at[1]),
    ]

    @pl.when(pl.program_id(0) == 0)
    def _():
        for move in moves:
            move.start()

    full_a[...] = part_a[...].astype(jnp.float32) / count
    full_b[...] = part_b[...].astype(jnp.float32) / count

    @pl.when(pl.program_id(0) == steps - 1)
    def _():
        for move in moves:
            move.wait()


def finish(part_a, part_b, features, decoded, count):
    steps = 5
    away = pl.BlockSpec(memory_space=pl.ANY)
    rows = [pl.BlockSpec((part.shape[0] // steps, part.shape[1]), lambda i: (i, 0)) for part in (part_a, part_b)]
    return pl.pallas_call(
        functools.partial(finish_kernel, steps, float(count)),
        grid=(steps,),
        out_shape=(
            jax.ShapeDtypeStruct(part_a.shape, jnp.float32),
            jax.ShapeDtypeStruct(part_b.shape, jnp.float32),
            jax.ShapeDtypeStruct(features.shape, features.dtype),
            jax.ShapeDtypeStruct(decoded.shape, decoded.dtype),
        ),
        in_specs=rows + [away] * 2,
        out_specs=tuple(rows + [away] * 2),
        scratch_shapes=[pltpu.SemaphoreType.DMA((2,))],
    )(part_a, part_b, features, decoded)


def reducible(patches, width, inner, dec_width, scenes, tiles):
    return (
        scenes == 4
        and tiles == 8
        and inner == 2 * width
        and width % (tiles * 16) == 0
        and width % WIDE == 0
        and (width // tiles * 8) % WIDE == 0
        and inner % (width // tiles * 8) == 0
        and inner // (width // tiles * 8) == 2
        and patches % 256 == 0
        and width // tiles == 160
        and dec_width % LANES == 0
    )


def shards(
    features,
    visible,
    positions,
    cotangent,
    mlp_gain,
    mlp_bias,
    fc1_weight,
    fc1_bias,
    fc2_weight,
    fc2_bias,
    encoder_gain,
    encoder_bias,
    embed_weight,
    embed_bias,
    mask_token,
    position_table,
    decoder_gain,
    decoder_bias,
):
    patch_count = features.shape[2]
    model_width = features.shape[3]
    dec_width = embed_weight.shape[1]
    tiles = lax.axis_size("tile")
    scenes = lax.axis_size("dp")
    most_rows = patch_count // 2
    flags = visible.reshape(patch_count)
    row_data = features.reshape(patch_count, model_width)
    if reducible(
        patch_count, model_width, fc1_weight.shape[1], dec_width, scenes, tiles
    ):
        total_a, total_b, grad_rows, decoded = fused(
            row_data,
            cotangent.reshape(patch_count, dec_width),
            visible,
            positions,
            (fc1_weight, fc2_weight, embed_weight, position_table),
            (
                mlp_gain,
                mlp_bias,
                fc1_bias,
                fc2_bias,
                encoder_gain,
                encoder_bias,
                embed_bias,
                mask_token,
                decoder_gain,
                decoder_bias,
            ),
            tiles,
        )
        fc1_grad, fc2_grad, grad_rows, decoded = finish(
            total_a, total_b, grad_rows, decoded, scenes * tiles
        )
        return (
            grad_rows.reshape(features.shape),
            decoded.reshape(cotangent.shape),
            fc1_grad,
            fc2_grad,
        )
    keep_rows = (flags > 0)[:, None]
    upstream = cotangent.reshape(patch_count, dec_width)
    ids = jnp.arange(patch_count, dtype=jnp.int32)
    row_rank = jnp.sum(jnp.where(ids[None, :] < ids[:, None], flags[None, :], 0), axis=1)
    slots = jnp.arange(most_rows, dtype=jnp.int32)
    target = jnp.where(flags > 0, row_rank, -1)
    gather = (slots[:, None] == target[None, :]).astype(jnp.bfloat16)
    scatter = (target[:, None] == slots[None, :]).astype(jnp.bfloat16)
    enc_params = (
        mlp_gain,
        mlp_bias,
        fc1_weight,
        fc1_bias,
        fc2_weight,
        fc2_bias,
        encoder_gain,
        encoder_bias,
        embed_weight,
        embed_bias,
    )
    decoder_args = (position_table, mask_token, decoder_gain, decoder_bias)
    enc_input = jnp.dot(gather, row_data, preferred_element_type=jnp.bfloat16)
    saved, projected = encode(enc_input, enc_params)
    projected_rows = jnp.dot(scatter, projected, preferred_element_type=jnp.float32)
    decoded, grad_projected = decoder_pass(
        projected_rows, keep_rows, positions.reshape(-1), upstream, *decoder_args
    )
    grad_compact = jnp.dot(gather, grad_projected, preferred_element_type=jnp.bfloat16)
    mlp_in, grad_pre, hidden, grad_encoded, grad_feats = encode_back(
        saved, grad_compact, enc_params
    )
    device_total = scenes * tiles
    grad_rows = jnp.dot(scatter, grad_feats, preferred_element_type=jnp.bfloat16)
    totals = []
    for left, right in ((mlp_in, grad_pre), (hidden, grad_encoded)):
        term = jnp.dot(left.T, right, preferred_element_type=jnp.float32)
        share = lax.psum_scatter(
            term.astype(jnp.bfloat16), "tile", scatter_dimension=0, tiled=True
        )
        totals.append(lax.psum(share, "dp").astype(jnp.float32))
    fc1_grad, fc2_grad = [total / device_total for total in totals]
    feature_grad = grad_rows.reshape(features.shape)
    decoded_out = decoded.reshape(cotangent.shape)
    return (feature_grad, decoded_out, fc1_grad, fc2_grad)


def solution(mesh):
    return jax.shard_map(
        shards,
        mesh=mesh,
        in_specs=(
            P("dp", "tile", None, None),
            P("dp", "tile", None),
            P("dp", "tile", None),
            P("dp", "tile", None, None),
            P(),
            P(),
            P(),
            P(),
            P(),
            P(),
            P(),
            P(),
            P(),
            P(),
            P(),
            P(),
            P(),
            P(),
        ),
        out_specs=(
            P("dp", "tile", None, None),
            P("dp", "tile", None, None),
            P("tile", None),
            P("tile", None),
        ),
        check_vma=False,
    )
```

```python
import functools

import jax
import jax.numpy as jnp
from jax import lax
from jax.experimental import pallas as pl
from jax.experimental.pallas import tpu as pltpu
from jax.sharding import PartitionSpec as P

MESH = pl.DeviceIdType.MESH

epsilon = 1e-06


def layer_norm(values, norm_gain, norm_bias):
    row_mean = jnp.mean(values, axis=-1, keepdims=True)
    centred = values - row_mean
    variance = jnp.mean(centred * centred, axis=-1, keepdims=True)
    inv_std = lax.rsqrt(variance + epsilon)
    scaled = centred * inv_std
    return (scaled * norm_gain + norm_bias, scaled, inv_std)


def norm_back(upstream, scaled, inv_std):
    mean_up = jnp.mean(upstream, axis=-1, keepdims=True)
    mean_cross = jnp.mean(upstream * scaled, axis=-1, keepdims=True)
    return inv_std * (upstream - mean_up - scaled * mean_cross)


def gelu_parts(pre_act):
    normal_cdf = 0.5 * (1.0 + lax.erf(pre_act * 0.7071067811865476))
    density = jnp.exp(-0.5 * pre_act * pre_act) * 0.3989422804014327
    return (pre_act * normal_cdf, normal_cdf + pre_act * density)


def encode(enc_input, enc_params):
    (
        mlp_gain,
        mlp_bias,
        fc1_weight,
        fc1_bias,
        fc2_weight,
        fc2_bias,
        encoder_gain,
        encoder_bias,
        embed_weight,
        embed_bias,
    ) = enc_params
    rows_in = enc_input.astype(jnp.float32)
    mlp_in, mlp_scaled, mlp_inv = layer_norm(rows_in, mlp_gain, mlp_bias)
    mlp_in = mlp_in.astype(jnp.bfloat16)
    pre_act = jnp.dot(mlp_in, fc1_weight, preferred_element_type=jnp.float32) + fc1_bias
    activation, slope = gelu_parts(pre_act)
    hidden = activation.astype(jnp.bfloat16)
    encoded = rows_in + jnp.dot(hidden, fc2_weight, preferred_element_type=jnp.float32) + fc2_bias
    normed, enc_scaled, enc_inv = layer_norm(encoded, encoder_gain, encoder_bias)
    normed = normed.astype(jnp.bfloat16)
    projected = (
        jnp.dot(normed, embed_weight, preferred_element_type=jnp.float32) + embed_bias
    ).astype(jnp.bfloat16)
    saved = (mlp_in, mlp_scaled, mlp_inv, slope, hidden, enc_scaled, enc_inv)
    return (saved, projected)


def encode_back(saved, grad_compact, enc_params):
    (
        mlp_gain,
        mlp_bias,
        fc1_weight,
        fc1_bias,
        fc2_weight,
        fc2_bias,
        encoder_gain,
        encoder_bias,
        embed_weight,
        embed_bias,
    ) = enc_params
    mlp_in, mlp_scaled, mlp_inv, slope, hidden, enc_scaled, enc_inv = saved
    grad_normed = jnp.dot(grad_compact, embed_weight.T, preferred_element_type=jnp.float32)
    grad_encoded = norm_back(grad_normed * encoder_gain, enc_scaled, enc_inv).astype(jnp.bfloat16)
    grad_hidden = jnp.dot(grad_encoded, fc2_weight.T, preferred_element_type=jnp.float32)
    grad_pre = (grad_hidden * slope).astype(jnp.bfloat16)
    grad_mlp_in = jnp.dot(grad_pre, fc1_weight.T, preferred_element_type=jnp.float32)
    grad_feats = (
        grad_encoded.astype(jnp.float32) + norm_back(grad_mlp_in * mlp_gain, mlp_scaled, mlp_inv)
    ).astype(jnp.bfloat16)
    return (mlp_in, grad_pre, hidden, grad_encoded, grad_feats)


def decoder_pass(
    projected_rows,
    keep_rows,
    position_ids,
    upstream,
    position_table,
    mask_token,
    decoder_gain,
    decoder_bias,
):
    table_ids = jnp.arange(position_table.shape[0], dtype=jnp.int32)[None, :]
    pick = (position_ids[:, None] == table_ids).astype(jnp.bfloat16)
    placed = jnp.dot(pick, position_table, preferred_element_type=jnp.float32)
    dec_input = jnp.where(keep_rows, projected_rows, mask_token) + placed
    decoded, dec_scaled, dec_inv = layer_norm(dec_input, decoder_gain, decoder_bias)
    grad_input = norm_back(upstream.astype(jnp.float32) * decoder_gain, dec_scaled, dec_inv)
    grad_projected = jnp.where(keep_rows, grad_input, 0.0).astype(jnp.bfloat16)
    return (decoded.astype(jnp.bfloat16), grad_projected)


LANES = 128
WIDE = 256


def normalize(values):
    row_mean = jnp.mean(values, axis=-1, keepdims=True)
    centred = values - row_mean
    variance = jnp.mean(centred * centred, axis=-1, keepdims=True)
    inv_std = lax.rsqrt(variance + epsilon)
    return (centred * inv_std, inv_std)


def nt_dot(left, right):
    return lax.dot_general(
        left, right, (((1,), (1,)), ((), ())), preferred_element_type=jnp.float32
    )


def nn_dot(left, right):
    return jnp.dot(left, right, preferred_element_type=jnp.float32)


def fused_kernel(
    chunks,
    z_count,
    visible,
    positions,
    mlp_gain,
    mlp_bias,
    fc1_bias,
    fc2_bias,
    encoder_gain,
    encoder_bias,
    embed_bias,
    mask_token,
    decoder_gain,
    decoder_bias,
    features,
    cotangent,
    fc1_weight,
    fc2_weight,
    embed_weight,
    position_table,
    out_a,
    out_b,
    feature_out,
    decoded_out,
    vectors,
    feats,
    cot,
    fc1,
    fc2,
    embed,
    table,
    gather,
    scatter,
    rows_in,
    mlp_scaled,
    mlp_inv,
    mlp_in,
    hidden,
    slope,
    by_half,
    encoded,
    enc_inv,
    normed,
    projected,
    placed,
    placed_rows,
    cot_rows,
    grad_rows,
    upstream,
    grad_encoded,
    grad_pre,
    turned_a,
    turned_b,
    rhs_cat_a,
    rhs_cat_b,
    gathered_a,
    gathered_b,
    acc_a,
    acc_b,
    core_send_a,
    core_send_b,
    core_land_a,
    core_land_b,
    half_send_a,
    half_send_b,
    half_land_a,
    half_land_b,
    near_send_a,
    near_send_b,
    near_land_a,
    near_land_b,
    far_send_a,
    far_send_b,
    far_land_a,
    far_land_b,
    load_sems,
    early_sems,
    late_sems,
    pair_sems,
    spread_sems,
):
    half_type, full_type = jnp.bfloat16, jnp.float32
    for row, vector in enumerate(
        (
            mlp_gain,
            mlp_bias,
            fc1_bias,
            fc2_bias,
            encoder_gain,
            encoder_bias,
            embed_bias,
            mask_token,
            decoder_gain,
            decoder_bias,
        )
    ):
        vectors[row : row + 1, 0 : vector.shape[0]] = vector[...].reshape(1, -1)
    (
        mlp_gain,
        mlp_bias,
        fc1_bias,
        fc2_bias,
        encoder_gain,
        encoder_bias,
        embed_bias,
        mask_token,
        decoder_gain,
        decoder_bias,
    ) = [
        vectors.at[row : row + 1, 0 : vector.shape[0]]
        for row, vector in enumerate(
            (
                mlp_gain,
                mlp_bias,
                fc1_bias,
                fc2_bias,
                encoder_gain,
                encoder_bias,
                embed_bias,
                mask_token,
                decoder_gain,
                decoder_bias,
            )
        )
    ]
    dp = lax.axis_index("dp")
    tile = lax.axis_index("tile")
    x = lax.rem(dp, 2)
    y = lax.div(dp, 2)
    core = lax.rem(tile, 2)
    my_z = lax.div(tile, 2)
    sibling = (dp, tile + 1 - 2 * core)
    across_x = (dp + 1 - 2 * x, tile)
    across_y = (dp + 2 - 4 * y, tile)
    diagonal = (3 - dp, tile)
    z_low, z_high = lax.rem(my_z, 2), lax.div(my_z, 2)
    near_z = (dp, tile + 2 - 4 * z_low)
    far_z = (dp, tile + 4 - 8 * z_high)
    peers = [sibling, across_x, across_y, diagonal, near_z, far_z]

    barrier = pltpu.get_barrier_semaphore()
    for peer in peers:
        pl.semaphore_signal(barrier, inc=1, device_id=peer, device_id_type=MESH)
    halves = fc1.shape[1] // 2
    load_feats = pltpu.make_async_copy(features, feats, load_sems.at[0])
    load_fc1 = [
        pltpu.make_async_copy(
            fc1_weight.at[:, k * halves : (k + 1) * halves],
            fc1.at[:, k * halves : (k + 1) * halves],
            load_sems.at[1 + k],
        )
        for k in range(2)
    ]
    load_table = pltpu.make_async_copy(position_table, table, load_sems.at[3])
    load_cot = pltpu.make_async_copy(cotangent, cot, load_sems.at[4])
    load_embed = pltpu.make_async_copy(embed_weight, embed, load_sems.at[5])
    load_fc2 = pltpu.make_async_copy(fc2_weight, fc2, load_sems.at[6])
    for load in (load_feats, load_fc1[0], load_table, load_cot):
        load.start()

    patches, width = feats.shape
    batch, inner = hidden.shape
    piece = turned_a.shape[2] // z_count
    block = 2 * piece
    half = chunks * LANES
    turned = (turned_a, turned_b)
    rhs = (grad_pre, grad_encoded)
    rhs_cat = (rhs_cat_a, rhs_cat_b)
    gathered = (gathered_a, gathered_b)
    acc = (acc_a, acc_b)
    core_send, core_land = (core_send_a, core_send_b), (core_land_a, core_land_b)
    half_send, half_land = (half_send_a, half_send_b), (half_land_a, half_land_b)
    near_send, near_land = (near_send_a, near_send_b), (near_land_a, near_land_b)
    far_send, far_land = (far_send_a, far_send_b), (far_land_a, far_land_b)
    gather_peer = (across_x, across_y)
    half_peer = (across_y, across_x)
    kept = (y, x)
    own_base = (x * 2 * half, 0)
    far_base = ((1 - x) * 2 * half, 0)
    copies = {}

    def send(key, src, dst, sems, at, peer):
        copy = pltpu.make_async_remote_copy(
            src_ref=src,
            dst_ref=dst,
            send_sem=sems.at[(0,) + at],
            recv_sem=sems.at[(1,) + at],
            device_id=peer,
            device_id_type=MESH,
        )
        copy.start()
        copies[key] = copy

    def row_blocks(count, tall, body):
        @pl.loop(0, count)
        def _(i):
            body(pl.ds(pl.multiple_of(i * tall, tall), tall))

    def each_block(count, tall, body):
        for i in range(count):
            body(slice(i * tall, (i + 1) * tall))

    def column_blocks(count, body):
        @pl.loop(0, count)
        def _(i):
            body(pl.ds(pl.multiple_of(i * WIDE, WIDE), WIDE))

    flags = visible[...] > 0
    ones = jnp.broadcast_to(jnp.where(flags, 1.0, 0.0), (16, patches)).astype(half_type)
    before = lax.broadcasted_iota(jnp.int32, (patches, patches), 0) < lax.broadcasted_iota(
        jnp.int32, (patches, patches), 1
    )
    rank = nn_dot(ones, jnp.where(before, 1.0, 0.0).astype(half_type))[0:1, :]
    target = jnp.where(flags, rank, -1.0).astype(jnp.int32)
    slot = lax.broadcasted_iota(jnp.int32, (batch, patches), 0)
    gather[...] = jnp.where(slot == target, 1.0, 0.0).astype(half_type)
    load_feats.wait()
    load_fc1[1].start()

    def compact(at):
        rows_in[:, at] = nn_dot(gather[...], feats[:, at]).astype(half_type)

    each_block(width // WIDE, WIDE, compact)

    def first_norm(at):
        scaled, inverse = normalize(rows_in[at, :].astype(full_type))
        mlp_scaled[at, :] = scaled
        mlp_inv[at, :] = inverse
        mlp_in[at, :] = (scaled * mlp_gain[...] + mlp_bias[...]).astype(half_type)

    each_block(batch // 32, 32, first_norm)
    for at in range(0, width, WIDE):
        flipped = mlp_in[:, at : at + WIDE].T
        row = at
        while row < at + WIDE:
            number, upper = row // block, row // piece
            stop = min(at + WIDE, (upper + 1) * piece)
            first = (number // 2) * piece + row - upper * piece
            turned_a[number % 2, upper % 2, first : first + stop - row, 0:batch] = flipped[
                row - at : stop - at
            ]
            row = stop
    load_fc2.start()
    load_embed.start()
    pl.semaphore_wait(barrier, len(peers))
    send(
        ("e", 0, 0),
        turned_a.at[:, :, :, 0:batch],
        turned_a.at[:, :, :, batch : 2 * batch],
        early_sems,
        (0, 0),
        across_x,
    )

    load_table.wait()
    load_cot.wait()
    names = lax.broadcasted_iota(jnp.int32, (patches, patches), 0)
    pick = jnp.where(names == positions[...], 1.0, 0.0).astype(half_type).T
    placed[...] = nn_dot(pick, table[...]).astype(half_type)
    placed_rows[...] = nn_dot(gather[...], placed[...]).astype(half_type)
    cot_rows[...] = nn_dot(gather[...], cot[...]).astype(half_type)
    group = 8 * block
    for i in range(inner // group):
        load_fc1[i].wait()
        for at in range(0, group, WIDE):
            columns = slice(i * group + at, i * group + at + WIDE)
            pre_act = nn_dot(mlp_in[...], fc1[:, columns]) + fc1_bias[:, columns]
            activation, slope[:, columns] = gelu_parts(pre_act)
            activation = activation.astype(half_type)
            hidden[:, columns] = activation
            flipped = activation.T
            row = at
            while row < at + WIDE:
                number, upper = row // block, row // piece
                stop = min(at + WIDE, (upper + 1) * piece)
                first = (2 * i + number // 4) * piece + row - upper * piece
                by_half[
                    number % 2, (number // 2) % 2, upper % 2, first : first + stop - row, :
                ] = flipped[row - at : stop - at]
                row = stop
        part = slice(2 * i * piece, 2 * (i + 1) * piece)
        send(
            ("e", 1, i),
            by_half.at[1 - y, :, :, part, :],
            turned_b.at[:, :, part, batch : 2 * batch],
            early_sems,
            (1, i),
            across_y,
        )
    turned_b[:, :, :, 0:batch] = by_half[y]

    load_fc2.wait()

    def second_product(at):
        encoded[:, at] = (
            rows_in[:, at].astype(full_type) + nn_dot(hidden[...], fc2[:, at]) + fc2_bias[:, at]
        )

    column_blocks(width // WIDE, second_product)

    def second_norm(at):
        scaled, inverse = normalize(encoded[at, :])
        encoded[at, :] = scaled
        enc_inv[at, :] = inverse
        normed[at, :] = (scaled * encoder_gain[...] + encoder_bias[...]).astype(half_type)

    each_block(batch // 32, 32, second_norm)
    load_embed.wait()
    projected[...] = (nn_dot(normed[...], embed[...]) + embed_bias[...]).astype(half_type)

    def decoder_rows(at):
        scaled, inverse = normalize(
            projected[at, :].astype(full_type) + placed_rows[at, :].astype(full_type)
        )
        back = norm_back(cot_rows[at, :].astype(full_type) * decoder_gain[...], scaled, inverse)
        grad_rows[at, :] = back.astype(half_type)

    each_block(batch // 32, 32, decoder_rows)

    def embed_back(at):
        upstream[:, at] = nt_dot(grad_rows[...], embed[at, :]) * encoder_gain[:, at]

    each_block(width // WIDE, WIDE, embed_back)

    def encoder_back(at):
        grad_encoded[at, :] = norm_back(upstream[at, :], encoded[at, :], enc_inv[at, :]).astype(
            half_type
        )

    each_block(batch // 32, 32, encoder_back)

    def late(t, j):
        for h in range(2):
            first = pl.multiple_of(far_base[t] + h * half + j * LANES, LANES)
            send(
                ("l", t, j, h),
                rhs[t].at[:, pl.ds(first, LANES)],
                rhs_cat[t].at[j, batch : 2 * batch, h * LANES : (h + 1) * LANES],
                late_sems,
                (t, j, h),
                gather_peer[t],
            )

    def pre_columns(base, j, own):
        at = [
            pl.ds(pl.multiple_of(base + h * half + j * LANES, LANES), LANES) for h in range(2)
        ]
        weights = jnp.concatenate([fc2[at[0], :], fc2[at[1], :]], axis=0)
        part = nt_dot(grad_encoded[...], weights)
        for h in range(2):
            value = (part[:, h * LANES : (h + 1) * LANES] * slope[:, at[h]]).astype(half_type)
            grad_pre[:, at[h]] = value
            if own:
                rhs_cat_a[j, 0:batch, h * LANES : (h + 1) * LANES] = value

    ahead = 1
    relayed = 2 * chunks - 2
    for j in range(ahead):
        late(1, j)
    for j in range(chunks):
        pre_columns(far_base[0], j, False)
        if j < ahead:
            late(0, j)
    for j in range(chunks):
        pre_columns(own_base[0], j, True)

    def feature_columns(at):
        upstream[:, at] = nt_dot(grad_pre[...], fc1[at, :]) * mlp_gain[:, at]

    def feature_rows(at):
        back = norm_back(upstream[at, :], mlp_scaled[at, :], mlp_inv[at, :])
        normed[at, :] = (grad_encoded[at, :].astype(full_type) + back).astype(half_type)

    def feature_place(at):
        feats[at, :] = nn_dot(scatter[at, :], normed[...]).astype(half_type)

    def decoder_place(at):
        picks = scatter[at, :]
        keep_rows = jnp.sum(picks.astype(full_type), axis=1, keepdims=True) > 0.5
        rows = jnp.where(keep_rows, nn_dot(picks, projected[...]), mask_token[...])
        scaled, _ = normalize(rows + placed[at, :].astype(full_type))
        cot[at, :] = (scaled * decoder_gain[...] + decoder_bias[...]).astype(half_type)

    stores = []

    def store(k, source, target):
        copy = pltpu.make_async_copy(source, target, load_sems.at[k])
        copy.start()
        stores.append(copy)

    def feature_part(k):
        if k == 0:
            each_block(patches // 64, 64, decoder_place)
            store(0, cot, decoded_out)
        if k == 1:
            column_blocks(width // WIDE, feature_columns)
        if k == 2:
            scatter[...] = gather[...].T
            each_block(batch // 32, 32, feature_rows)
            row_blocks(patches // 128, 128, feature_place)
            store(1, feats, feature_out)

    def products(t, n, which, put):
        part = nn_dot(turned[t][which, n % 2], rhs_cat[t][n // 2])
        for z in range(z_count):
            for h in range(2):
                put(
                    h,
                    z,
                    part[z * piece : (z + 1) * piece, h * LANES : (h + 1) * LANES],
                )

    def stage0(t, n):
        def put_send(h, z, value):
            core_send[t][n % 2, h, z] = value.astype(half_type)

        def put_own(h, z, value):
            acc[t][n, h, z] = value

        j = n // 2
        if n == 0:
            for i in range(1 if t == 0 else inner // group):
                copies["e", t, i].wait()
        if n % 2 == 0:
            if t == 1:
                for h in range(2):
                    first = pl.multiple_of(h * half + j * LANES, LANES)
                    rhs_cat_b[j, 0:batch, h * LANES : (h + 1) * LANES] = grad_encoded[
                        :, pl.ds(first, LANES)
                    ]
            for h in range(2):
                copies["l", t, j, h].wait()
        products(t, n, 1 - core, put_send)
        send(
            ("c", t, n), core_send[t].at[n % 2], core_land[t].at[n], pair_sems, (0, t, n), sibling
        )
        products(t, n, core, put_own)

    def stage1(t, n):
        r = kept[t]
        copies["c", t, n].wait()
        half_send[t][n % 2] = (
            acc[t][n, 1 - r] + core_land[t][n, 1 - r].astype(full_type)
        ).astype(half_type)
        send(
            ("h", t, n),
            half_send[t].at[n % 2],
            half_land[t].at[n],
            pair_sems,
            (1, t, n),
            half_peer[t],
        )
        acc[t][n, r] = acc[t][n, r] + core_land[t][n, r].astype(full_type)

    def stage2(t, n):
        r = kept[t]
        copies["h", t, n].wait()
        for e in range(2):
            z = 2 * e + 1 - z_low
            near_send[t][n % 2, e] = (
                acc[t][n, r, z] + half_land[t][n, z].astype(full_type)
            ).astype(half_type)
        send(
            ("n", t, n), near_send[t].at[n % 2], near_land[t].at[n], pair_sems, (2, t, n), near_z
        )
        for e in range(2):
            z = 2 * e + z_low
            acc[t][n, r, z] = acc[t][n, r, z] + half_land[t][n, z].astype(full_type)

    def stage3(t, n):
        r = kept[t]
        copies["n", t, n].wait()
        z = z_low + 2 * (1 - z_high)
        far_send[t][n % 2] = (
            acc[t][n, r, z] + near_land[t][n, 1 - z_high].astype(full_type)
        ).astype(half_type)
        send(("f", t, n), far_send[t].at[n % 2], far_land[t].at[n], pair_sems, (3, t, n), far_z)
        acc[t][n, r, my_z] = acc[t][n, r, my_z] + near_land[t][n, z_high].astype(full_type)

    def stage4(t, n):
        copies["f", t, n].wait()
        mine = 2 * x + y
        gathered[t][mine, n] = (
            acc[t][n, kept[t], my_z] + far_land[t][n].astype(full_type)
        ).astype(half_type)
        ways = (across_x, across_y, diagonal) if n >= relayed else (across_x, across_y)
        for k, peer in enumerate(ways):
            send(
                ("s", t, n, k),
                gathered[t].at[mine, n],
                gathered[t].at[mine, n],
                spread_sems,
                (t, n, k),
                peer,
            )

    def stage5(t, n):
        for k in range(2):
            copies["s", t, n, k].wait()
        if n >= relayed:
            return
        owner, peer = ((2 * (1 - x) + y, across_y), (2 * x + 1 - y, across_x))[n % 2]
        passed = gathered[t].at[owner, n]
        send(("s", t, n, 2), passed, passed, spread_sems, (t, n, 2), peer)

    def stage6(t, n):
        copies["s", t, n, 2].wait()
        j, low = n // 2, (n % 2) * piece
        for mine in range(4):
            if t == 0:
                first = mine * half + j * LANES
                out_a[low : low + piece, first : first + LANES] = gathered[t][mine, n]
            else:
                row, first = (mine % 2) * block + low, (mine // 2) * half + j * LANES
                out_b[row : row + piece, first : first + LANES] = gathered[t][mine, n]

    feature_part(1)
    feature_part(2)
    feature_part(0)
    items = [(t, n) for n in range(2 * chunks) for t in (0, 1)]
    stages = (
        (stage6, 22),
        (stage5, 18),
        (stage4, 14),
        (stage3, 10),
        (stage2, 6),
        (stage1, 2),
        (stage0, 0),
    )
    for step in range(len(items) + 22):
        if step < len(items):
            t, n = items[step]
            if n % 2 == 0 and n // 2 + ahead < chunks:
                late(t, n // 2 + ahead)
        for stage, lag in stages:
            i = step - lag
            if 0 <= i < len(items):
                stage(*items[i])
    for copy in stores:
        copy.wait()


def fused(row_data, upstream_rows, visible, positions, matrices, vectors, tiles):
    patches, width = row_data.shape
    fc1_weight, fc2_weight, embed_weight, position_table = matrices
    inner, dec_width = fc1_weight.shape[1], embed_weight.shape[1]
    rows = patches // 2
    z_count = tiles // 2
    block = width // tiles
    piece = block // 2
    chunks = width // 2 // LANES
    whole = pl.BlockSpec(memory_space=pltpu.VMEM)
    away = pl.BlockSpec(memory_space=pl.ANY)
    half, full = jnp.bfloat16, jnp.float32
    shapes = [
        ((16, inner), full),
        ((patches, width), half),
        ((patches, dec_width), half),
        (fc1_weight.shape, half),
        (fc2_weight.shape, half),
        (embed_weight.shape, half),
        (position_table.shape, half),
        ((rows, patches), half),
        ((patches, rows), half),
        ((rows, width), half),
        ((rows, width), full),
        ((rows, 1), full),
        ((rows, width), half),
        ((rows, inner), half),
        ((rows, inner), full),
        ((2, 2, 2, z_count * piece, rows), half),
        ((rows, width), full),
        ((rows, 1), full),
        ((rows, width), half),
        ((rows, dec_width), half),
        ((patches, dec_width), half),
        ((rows, dec_width), half),
        ((rows, dec_width), half),
        ((rows, dec_width), half),
        ((rows, width), full),
        ((rows, width), half),
        ((rows, inner), half),
    ]
    for lead, kind in (
        ((2, 2, z_count * piece, 2 * rows), half),
        ((chunks, 2 * rows, 2 * LANES), half),
        ((4, 2 * chunks, piece, LANES), half),
        ((2 * chunks, 2, z_count, piece, LANES), full),
        ((2, 2, z_count, piece, LANES), half),
        ((2 * chunks, 2, z_count, piece, LANES), half),
        ((2, z_count, piece, LANES), half),
        ((2 * chunks, z_count, piece, LANES), half),
        ((2, 2, piece, LANES), half),
        ((2 * chunks, 2, piece, LANES), half),
        ((2, piece, LANES), half),
        ((2 * chunks, piece, LANES), half),
    ):
        shapes += [(lead, kind)] * 2
    scratch = [pltpu.VMEM(lead, kind) for lead, kind in shapes]
    scratch += [
        pltpu.SemaphoreType.DMA((7,)),
        pltpu.SemaphoreType.DMA((2, 2, 2)),
        pltpu.SemaphoreType.DMA((2, 2, chunks, 2)),
        pltpu.SemaphoreType.DMA((2, 4, 2, 2 * chunks)),
        pltpu.SemaphoreType.DMA((2, 2, 2 * chunks, 3)),
    ]
    return pl.pallas_call(
        functools.partial(fused_kernel, chunks, z_count),
        out_shape=(
            jax.ShapeDtypeStruct((block, inner), half),
            jax.ShapeDtypeStruct((2 * block, width), half),
            jax.ShapeDtypeStruct((patches, width), half),
            jax.ShapeDtypeStruct((patches, dec_width), half),
        ),
        in_specs=[whole] * 12 + [away] * 6,
        out_specs=(whole, whole, away, away),
        scratch_shapes=scratch,
        compiler_params=pltpu.CompilerParams(
            collective_id=0, has_side_effects=True, vmem_limit_bytes=60 * 2**20
        ),
    )(
        visible.reshape(1, patches),
        positions.reshape(1, patches),
        *vectors,
        row_data,
        upstream_rows,
        fc1_weight,
        fc2_weight,
        embed_weight,
        position_table,
    )


def finish_kernel(
    count,
    part_a,
    part_b,
    features,
    decoded,
    full_a,
    full_b,
    feature_out,
    decoded_out,
    held_a,
    held_b,
    held_features,
    held_decoded,
    wide_a,
    wide_b,
    read_sems,
    write_sems,
):
    reads = []
    for k, (source, held) in enumerate(
        (
            (features, held_features),
            (part_a, held_a),
            (part_b, held_b),
            (decoded, held_decoded),
        )
    ):
        reads.append(pltpu.make_async_copy(source, held, read_sems.at[k]))
        reads[-1].start()
    writes = []
    for k, (held, target) in enumerate(
        (
            (held_features, feature_out),
            (wide_a, full_a),
            (wide_b, full_b),
            (held_decoded, decoded_out),
        )
    ):
        reads[k].wait()
        if k == 1:
            wide_a[...] = held_a[...].astype(jnp.float32) / count
        if k == 2:
            wide_b[...] = held_b[...].astype(jnp.float32) / count
        writes.append(pltpu.make_async_copy(held, target, write_sems.at[k]))
        writes[-1].start()
    for write in writes:
        write.wait()


def finish(part_a, part_b, features, decoded, count):
    away = pl.BlockSpec(memory_space=pl.ANY)
    parts = (part_a, part_b, features, decoded)
    kinds = (jnp.float32, jnp.float32, features.dtype, decoded.dtype)
    return pl.pallas_call(
        functools.partial(finish_kernel, float(count)),
        out_shape=tuple(
            jax.ShapeDtypeStruct(part.shape, kind) for part, kind in zip(parts, kinds)
        ),
        in_specs=[away] * 4,
        out_specs=(away,) * 4,
        scratch_shapes=[pltpu.VMEM(part.shape, part.dtype) for part in parts]
        + [pltpu.VMEM(part.shape, jnp.float32) for part in parts[:2]]
        + [pltpu.SemaphoreType.DMA((4,))] * 2,
        compiler_params=pltpu.CompilerParams(vmem_limit_bytes=32 * 2**20),
    )(*parts)


def reducible(patches, width, inner, dec_width, scenes, tiles):
    return (
        scenes == 4
        and tiles == 8
        and inner == 2 * width
        and width % (tiles * 16) == 0
        and width % WIDE == 0
        and (width // tiles * 8) % WIDE == 0
        and inner % (width // tiles * 8) == 0
        and inner // (width // tiles * 8) == 2
        and patches % 256 == 0
        and width // tiles == 160
        and dec_width % (4 * LANES) == 0
    )


def shards(
    features,
    visible,
    positions,
    cotangent,
    mlp_gain,
    mlp_bias,
    fc1_weight,
    fc1_bias,
    fc2_weight,
    fc2_bias,
    encoder_gain,
    encoder_bias,
    embed_weight,
    embed_bias,
    mask_token,
    position_table,
    decoder_gain,
    decoder_bias,
):
    patch_count = features.shape[2]
    model_width = features.shape[3]
    dec_width = embed_weight.shape[1]
    tiles = lax.axis_size("tile")
    scenes = lax.axis_size("dp")
    most_rows = patch_count // 2
    flags = visible.reshape(patch_count)
    row_data = features.reshape(patch_count, model_width)
    if reducible(
        patch_count, model_width, fc1_weight.shape[1], dec_width, scenes, tiles
    ):
        total_a, total_b, grad_rows, decoded = fused(
            row_data,
            cotangent.reshape(patch_count, dec_width),
            visible,
            positions,
            (fc1_weight, fc2_weight, embed_weight, position_table),
            (
                mlp_gain,
                mlp_bias,
                fc1_bias,
                fc2_bias,
                encoder_gain,
                encoder_bias,
                embed_bias,
                mask_token,
                decoder_gain,
                decoder_bias,
            ),
            tiles,
        )
        fc1_grad, fc2_grad, grad_rows, decoded = finish(
            total_a, total_b, grad_rows, decoded, scenes * tiles
        )
        return (
            grad_rows.reshape(features.shape),
            decoded.reshape(cotangent.shape),
            fc1_grad,
            fc2_grad,
        )
    keep_rows = (flags > 0)[:, None]
    upstream = cotangent.reshape(patch_count, dec_width)
    ids = jnp.arange(patch_count, dtype=jnp.int32)
    row_rank = jnp.sum(jnp.where(ids[None, :] < ids[:, None], flags[None, :], 0), axis=1)
    slots = jnp.arange(most_rows, dtype=jnp.int32)
    target = jnp.where(flags > 0, row_rank, -1)
    gather = (slots[:, None] == target[None, :]).astype(jnp.bfloat16)
    scatter = (target[:, None] == slots[None, :]).astype(jnp.bfloat16)
    enc_params = (
        mlp_gain,
        mlp_bias,
        fc1_weight,
        fc1_bias,
        fc2_weight,
        fc2_bias,
        encoder_gain,
        encoder_bias,
        embed_weight,
        embed_bias,
    )
    decoder_args = (position_table, mask_token, decoder_gain, decoder_bias)
    enc_input = jnp.dot(gather, row_data, preferred_element_type=jnp.bfloat16)
    saved, projected = encode(enc_input, enc_params)
    projected_rows = jnp.dot(scatter, projected, preferred_element_type=jnp.float32)
    decoded, grad_projected = decoder_pass(
        projected_rows, keep_rows, positions.reshape(-1), upstream, *decoder_args
    )
    grad_compact = jnp.dot(gather, grad_projected, preferred_element_type=jnp.bfloat16)
    mlp_in, grad_pre, hidden, grad_encoded, grad_feats = encode_back(
        saved, grad_compact, enc_params
    )
    device_total = scenes * tiles
    grad_rows = jnp.dot(scatter, grad_feats, preferred_element_type=jnp.bfloat16)
    totals = []
    for left, right in ((mlp_in, grad_pre), (hidden, grad_encoded)):
        term = jnp.dot(left.T, right, preferred_element_type=jnp.float32)
        share = lax.psum_scatter(
            term.astype(jnp.bfloat16), "tile", scatter_dimension=0, tiled=True
        )
        totals.append(lax.psum(share, "dp").astype(jnp.float32))
    fc1_grad, fc2_grad = [total / device_total for total in totals]
    feature_grad = grad_rows.reshape(features.shape)
    decoded_out = decoded.reshape(cotangent.shape)
    return (feature_grad, decoded_out, fc1_grad, fc2_grad)


def solution(mesh):
    return jax.shard_map(
        shards,
        mesh=mesh,
        in_specs=(
            P("dp", "tile", None, None),
            P("dp", "tile", None),
            P("dp", "tile", None),
            P("dp", "tile", None, None),
            P(),
            P(),
            P(),
            P(),
            P(),
            P(),
            P(),
            P(),
            P(),
            P(),
            P(),
            P(),
            P(),
            P(),
        ),
        out_specs=(
            P("dp", "tile", None, None),
            P("dp", "tile", None, None),
            P("tile", None),
            P("tile", None),
        ),
        check_vma=False,
    )
```

```python
import functools

import jax
import jax.numpy as jnp
from jax import lax
from jax.experimental import pallas as pl
from jax.experimental.pallas import tpu as pltpu
from jax.sharding import PartitionSpec as P

MESH = pl.DeviceIdType.MESH

epsilon = 1e-06


def layer_norm(values, norm_gain, norm_bias):
    row_mean = jnp.mean(values, axis=-1, keepdims=True)
    centred = values - row_mean
    variance = jnp.mean(centred * centred, axis=-1, keepdims=True)
    inv_std = lax.rsqrt(variance + epsilon)
    scaled = centred * inv_std
    return (scaled * norm_gain + norm_bias, scaled, inv_std)


def norm_back(upstream, scaled, inv_std):
    mean_up = jnp.mean(upstream, axis=-1, keepdims=True)
    mean_cross = jnp.mean(upstream * scaled, axis=-1, keepdims=True)
    return inv_std * (upstream - mean_up - scaled * mean_cross)


def gelu_parts(pre_act):
    normal_cdf = 0.5 * (1.0 + lax.erf(pre_act * 0.7071067811865476))
    density = jnp.exp(-0.5 * pre_act * pre_act) * 0.3989422804014327
    return (pre_act * normal_cdf, normal_cdf + pre_act * density)


def encode(enc_input, enc_params):
    (
        mlp_gain,
        mlp_bias,
        fc1_weight,
        fc1_bias,
        fc2_weight,
        fc2_bias,
        encoder_gain,
        encoder_bias,
        embed_weight,
        embed_bias,
    ) = enc_params
    rows_in = enc_input.astype(jnp.float32)
    mlp_in, mlp_scaled, mlp_inv = layer_norm(rows_in, mlp_gain, mlp_bias)
    mlp_in = mlp_in.astype(jnp.bfloat16)
    pre_act = jnp.dot(mlp_in, fc1_weight, preferred_element_type=jnp.float32) + fc1_bias
    activation, slope = gelu_parts(pre_act)
    hidden = activation.astype(jnp.bfloat16)
    encoded = rows_in + jnp.dot(hidden, fc2_weight, preferred_element_type=jnp.float32) + fc2_bias
    normed, enc_scaled, enc_inv = layer_norm(encoded, encoder_gain, encoder_bias)
    normed = normed.astype(jnp.bfloat16)
    projected = (
        jnp.dot(normed, embed_weight, preferred_element_type=jnp.float32) + embed_bias
    ).astype(jnp.bfloat16)
    saved = (mlp_in, mlp_scaled, mlp_inv, slope, hidden, enc_scaled, enc_inv)
    return (saved, projected)


def encode_back(saved, grad_compact, enc_params):
    (
        mlp_gain,
        mlp_bias,
        fc1_weight,
        fc1_bias,
        fc2_weight,
        fc2_bias,
        encoder_gain,
        encoder_bias,
        embed_weight,
        embed_bias,
    ) = enc_params
    mlp_in, mlp_scaled, mlp_inv, slope, hidden, enc_scaled, enc_inv = saved
    grad_normed = jnp.dot(grad_compact, embed_weight.T, preferred_element_type=jnp.float32)
    grad_encoded = norm_back(grad_normed * encoder_gain, enc_scaled, enc_inv).astype(jnp.bfloat16)
    grad_hidden = jnp.dot(grad_encoded, fc2_weight.T, preferred_element_type=jnp.float32)
    grad_pre = (grad_hidden * slope).astype(jnp.bfloat16)
    grad_mlp_in = jnp.dot(grad_pre, fc1_weight.T, preferred_element_type=jnp.float32)
    grad_feats = (
        grad_encoded.astype(jnp.float32) + norm_back(grad_mlp_in * mlp_gain, mlp_scaled, mlp_inv)
    ).astype(jnp.bfloat16)
    return (mlp_in, grad_pre, hidden, grad_encoded, grad_feats)


def decoder_pass(
    projected_rows,
    keep_rows,
    position_ids,
    upstream,
    position_table,
    mask_token,
    decoder_gain,
    decoder_bias,
):
    table_ids = jnp.arange(position_table.shape[0], dtype=jnp.int32)[None, :]
    pick = (position_ids[:, None] == table_ids).astype(jnp.bfloat16)
    placed = jnp.dot(pick, position_table, preferred_element_type=jnp.float32)
    dec_input = jnp.where(keep_rows, projected_rows, mask_token) + placed
    decoded, dec_scaled, dec_inv = layer_norm(dec_input, decoder_gain, decoder_bias)
    grad_input = norm_back(upstream.astype(jnp.float32) * decoder_gain, dec_scaled, dec_inv)
    grad_projected = jnp.where(keep_rows, grad_input, 0.0).astype(jnp.bfloat16)
    return (decoded.astype(jnp.bfloat16), grad_projected)


LANES = 128
WIDE = 256
RING = 3
FAR_RING = 6


def normalize(values):
    row_mean = jnp.mean(values, axis=-1, keepdims=True)
    centred = values - row_mean
    variance = jnp.mean(centred * centred, axis=-1, keepdims=True)
    inv_std = lax.rsqrt(variance + epsilon)
    return (centred * inv_std, inv_std)


def nt_dot(left, right):
    return lax.dot_general(
        left, right, (((1,), (1,)), ((), ())), preferred_element_type=jnp.float32
    )


def nn_dot(left, right):
    return jnp.dot(left, right, preferred_element_type=jnp.float32)


def fused_kernel(
    chunks,
    z_count,
    visible,
    positions,
    mlp_gain,
    mlp_bias,
    fc1_bias,
    fc2_bias,
    encoder_gain,
    encoder_bias,
    embed_bias,
    mask_token,
    decoder_gain,
    decoder_bias,
    features,
    cotangent,
    fc1_weight,
    fc2_weight,
    embed_weight,
    position_table,
    out_a,
    out_b,
    feature_out,
    decoded_out,
    vectors,
    feats,
    cot,
    fc1,
    fc2,
    embed,
    table,
    gather,
    scatter,
    rows_in,
    mlp_scaled,
    mlp_inv,
    mlp_in,
    hidden,
    slope,
    by_half,
    encoded,
    enc_inv,
    normed,
    projected,
    placed,
    placed_rows,
    cot_rows,
    grad_rows,
    upstream,
    grad_encoded,
    grad_pre,
    turned_a,
    turned_b,
    rhs_cat_a,
    rhs_cat_b,
    gathered_a,
    gathered_b,
    acc_a,
    acc_b,
    core_send_a,
    core_send_b,
    core_land_a,
    core_land_b,
    half_send_a,
    half_send_b,
    half_land_a,
    half_land_b,
    near_send_a,
    near_send_b,
    near_land_a,
    near_land_b,
    far_send_a,
    far_send_b,
    far_land_a,
    far_land_b,
    load_sems,
    early_sems,
    late_sems,
    pair_sems,
    spread_sems,
    out_sems,
):
    half_type, full_type = jnp.bfloat16, jnp.float32
    for row, vector in enumerate(
        (
            mlp_gain,
            mlp_bias,
            fc1_bias,
            fc2_bias,
            encoder_gain,
            encoder_bias,
            embed_bias,
            mask_token,
            decoder_gain,
            decoder_bias,
        )
    ):
        vectors[row : row + 1, 0 : vector.shape[0]] = vector[...].reshape(1, -1)
    (
        mlp_gain,
        mlp_bias,
        fc1_bias,
        fc2_bias,
        encoder_gain,
        encoder_bias,
        embed_bias,
        mask_token,
        decoder_gain,
        decoder_bias,
    ) = [
        vectors.at[row : row + 1, 0 : vector.shape[0]]
        for row, vector in enumerate(
            (
                mlp_gain,
                mlp_bias,
                fc1_bias,
                fc2_bias,
                encoder_gain,
                encoder_bias,
                embed_bias,
                mask_token,
                decoder_gain,
                decoder_bias,
            )
        )
    ]
    dp = lax.axis_index("dp")
    tile = lax.axis_index("tile")
    x = lax.rem(dp, 2)
    y = lax.div(dp, 2)
    core = lax.rem(tile, 2)
    my_z = lax.div(tile, 2)
    sibling = (dp, tile + 1 - 2 * core)
    across_x = (dp + 1 - 2 * x, tile)
    across_y = (dp + 2 - 4 * y, tile)
    diagonal = (3 - dp, tile)
    z_low, z_high = lax.rem(my_z, 2), lax.div(my_z, 2)
    near_z = (dp, tile + 2 - 4 * z_low)
    far_z = (dp, tile + 4 - 8 * z_high)
    peers = [sibling, across_x, across_y, diagonal, near_z, far_z]

    barrier = pltpu.get_barrier_semaphore()
    for peer in peers:
        pl.semaphore_signal(barrier, inc=1, device_id=peer, device_id_type=MESH)
    halves = fc1.shape[1] // 2
    load_feats = pltpu.make_async_copy(features, feats, load_sems.at[0])
    load_fc1 = [
        pltpu.make_async_copy(
            fc1_weight.at[:, k * halves : (k + 1) * halves],
            fc1.at[:, k * halves : (k + 1) * halves],
            load_sems.at[1 + k],
        )
        for k in range(2)
    ]
    load_table = pltpu.make_async_copy(position_table, table, load_sems.at[3])
    load_cot = pltpu.make_async_copy(cotangent, cot, load_sems.at[4])
    load_embed = pltpu.make_async_copy(embed_weight, embed, load_sems.at[5])
    load_fc2 = pltpu.make_async_copy(fc2_weight, fc2, load_sems.at[6])
    for load in (load_feats, load_fc1[0], load_table, load_cot):
        load.start()

    patches, width = feats.shape
    batch, inner = hidden.shape
    piece = turned_a.shape[2] // z_count
    block = 2 * piece
    half = chunks * LANES
    turned = (turned_a, turned_b)
    rhs = (grad_pre, grad_encoded)
    rhs_cat = (rhs_cat_a, rhs_cat_b)
    gathered = (gathered_a, gathered_b)
    acc = (acc_a, acc_b)
    core_send, core_land = (core_send_a, core_send_b), (core_land_a, core_land_b)
    half_send, half_land = (half_send_a, half_send_b), (half_land_a, half_land_b)
    near_send, near_land = (near_send_a, near_send_b), (near_land_a, near_land_b)
    far_send, far_land = (far_send_a, far_send_b), (far_land_a, far_land_b)
    gather_peer = (across_x, across_y)
    half_peer = (across_y, across_x)
    kept = (y, x)
    own_base = (x * 2 * half, 0)
    far_base = ((1 - x) * 2 * half, 0)
    copies = {}

    def send(key, src, dst, sems, at, peer):
        copy = pltpu.make_async_remote_copy(
            src_ref=src,
            dst_ref=dst,
            send_sem=sems.at[(0,) + at],
            recv_sem=sems.at[(1,) + at],
            device_id=peer,
            device_id_type=MESH,
        )
        copy.start()
        copies[key] = copy

    def row_blocks(count, tall, body):
        @pl.loop(0, count)
        def _(i):
            body(pl.ds(pl.multiple_of(i * tall, tall), tall))

    def each_block(count, tall, body):
        for i in range(count):
            body(slice(i * tall, (i + 1) * tall))

    def column_blocks(count, body):
        @pl.loop(0, count)
        def _(i):
            body(pl.ds(pl.multiple_of(i * WIDE, WIDE), WIDE))

    flags = visible[...] > 0
    ones = jnp.broadcast_to(jnp.where(flags, 1.0, 0.0), (16, patches)).astype(half_type)
    before = lax.broadcasted_iota(jnp.int32, (patches, patches), 0) < lax.broadcasted_iota(
        jnp.int32, (patches, patches), 1
    )
    rank = nn_dot(ones, jnp.where(before, 1.0, 0.0).astype(half_type))[0:1, :]
    target = jnp.where(flags, rank, -1.0).astype(jnp.int32)
    slot = lax.broadcasted_iota(jnp.int32, (batch, patches), 0)
    gather[...] = jnp.where(slot == target, 1.0, 0.0).astype(half_type)
    load_feats.wait()
    load_fc1[1].start()

    def compact(at):
        rows_in[:, at] = nn_dot(gather[...], feats[:, at]).astype(half_type)

    each_block(width // WIDE, WIDE, compact)

    def first_norm(at):
        scaled, inverse = normalize(rows_in[at, :].astype(full_type))
        mlp_scaled[at, :] = scaled
        mlp_inv[at, :] = inverse
        mlp_in[at, :] = (scaled * mlp_gain[...] + mlp_bias[...]).astype(half_type)

    each_block(batch // 32, 32, first_norm)
    for at in range(0, width, WIDE):
        flipped = mlp_in[:, at : at + WIDE].T
        row = at
        while row < at + WIDE:
            number, upper = row // block, row // piece
            stop = min(at + WIDE, (upper + 1) * piece)
            first = (number // 2) * piece + row - upper * piece
            turned_a[number % 2, upper % 2, first : first + stop - row, 0:batch] = flipped[
                row - at : stop - at
            ]
            row = stop
    pl.semaphore_wait(barrier, len(peers))
    send(
        ("e", 0, 0),
        turned_a.at[:, :, :, 0:batch],
        turned_a.at[:, :, :, batch : 2 * batch],
        early_sems,
        (0, 0),
        across_x,
    )

    load_fc2.start()
    load_embed.start()
    group = 8 * block
    for i in range(inner // group):
        load_fc1[i].wait()
        for at in range(0, group, WIDE):
            columns = slice(i * group + at, i * group + at + WIDE)
            pre_act = nn_dot(mlp_in[...], fc1[:, columns]) + fc1_bias[:, columns]
            activation, slope[:, columns] = gelu_parts(pre_act)
            activation = activation.astype(half_type)
            hidden[:, columns] = activation
            flipped = activation.T
            row = at
            while row < at + WIDE:
                number, upper = row // block, row // piece
                stop = min(at + WIDE, (upper + 1) * piece)
                first = (2 * i + number // 4) * piece + row - upper * piece
                by_half[
                    number % 2, (number // 2) % 2, upper % 2, first : first + stop - row, :
                ] = flipped[row - at : stop - at]
                row = stop
        part = slice(2 * i * piece, 2 * (i + 1) * piece)
        send(
            ("e", 1, i),
            by_half.at[1 - y, :, :, part, :],
            turned_b.at[:, :, part, batch : 2 * batch],
            early_sems,
            (1, i),
            across_y,
        )
    turned_b[:, :, :, 0:batch] = by_half[y]
    load_table.wait()
    load_cot.wait()
    names = lax.broadcasted_iota(jnp.int32, (patches, patches), 0)
    pick = jnp.where(names == positions[...], 1.0, 0.0).astype(half_type).T
    placed[...] = nn_dot(pick, table[...]).astype(half_type)
    placed_rows[...] = nn_dot(gather[...], placed[...]).astype(half_type)
    cot_rows[...] = nn_dot(gather[...], cot[...]).astype(half_type)

    load_fc2.wait()

    def second_product(at):
        encoded[:, at] = (
            rows_in[:, at].astype(full_type) + nn_dot(hidden[...], fc2[:, at]) + fc2_bias[:, at]
        )

    column_blocks(width // WIDE, second_product)

    def second_norm(at):
        scaled, inverse = normalize(encoded[at, :])
        encoded[at, :] = scaled
        enc_inv[at, :] = inverse
        normed[at, :] = (scaled * encoder_gain[...] + encoder_bias[...]).astype(half_type)

    each_block(batch // 32, 32, second_norm)
    load_embed.wait()
    projected[...] = (nn_dot(normed[...], embed[...]) + embed_bias[...]).astype(half_type)

    def decoder_rows(at):
        scaled, inverse = normalize(
            projected[at, :].astype(full_type) + placed_rows[at, :].astype(full_type)
        )
        back = norm_back(cot_rows[at, :].astype(full_type) * decoder_gain[...], scaled, inverse)
        grad_rows[at, :] = back.astype(half_type)

    each_block(batch // 32, 32, decoder_rows)

    def embed_back(at):
        upstream[:, at] = nt_dot(grad_rows[...], embed[at, :]) * encoder_gain[:, at]

    each_block(width // WIDE, WIDE, embed_back)

    def encoder_back(at):
        grad_encoded[at, :] = norm_back(upstream[at, :], encoded[at, :], enc_inv[at, :]).astype(
            half_type
        )

    each_block(batch // 32, 32, encoder_back)

    def late(t, j):
        for h in range(2):
            first = pl.multiple_of(far_base[t] + h * half + j * LANES, LANES)
            send(
                ("l", t, j, h),
                rhs[t].at[:, pl.ds(first, LANES)],
                rhs_cat[t].at[j, batch : 2 * batch, h * LANES : (h + 1) * LANES],
                late_sems,
                (t, j, h),
                gather_peer[t],
            )

    def pre_columns(base, j, own):
        at = [
            pl.ds(pl.multiple_of(base + h * half + j * LANES, LANES), LANES) for h in range(2)
        ]
        weights = jnp.concatenate([fc2[at[0], :], fc2[at[1], :]], axis=0)
        part = nt_dot(grad_encoded[...], weights)
        for h in range(2):
            value = (part[:, h * LANES : (h + 1) * LANES] * slope[:, at[h]]).astype(half_type)
            grad_pre[:, at[h]] = value
            if own:
                rhs_cat_a[j, 0:batch, h * LANES : (h + 1) * LANES] = value

    ahead = 1
    relayed = 2 * chunks - 2
    for j in range(ahead):
        late(1, j)
    for j in range(chunks):
        pre_columns(far_base[0], j, False)
        if j < ahead:
            late(0, j)
    for j in range(chunks):
        pre_columns(own_base[0], j, True)

    def feature_columns(at):
        upstream[:, at] = nt_dot(grad_pre[...], fc1[at, :]) * mlp_gain[:, at]

    def feature_rows(at):
        back = norm_back(upstream[at, :], mlp_scaled[at, :], mlp_inv[at, :])
        normed[at, :] = (grad_encoded[at, :].astype(full_type) + back).astype(half_type)

    def feature_place(at):
        feats[at, :] = nn_dot(scatter[at, :], normed[...]).astype(half_type)

    def decoder_place(at):
        picks = scatter[at, :]
        keep_rows = jnp.sum(picks.astype(full_type), axis=1, keepdims=True) > 0.5
        rows = jnp.where(keep_rows, nn_dot(picks, projected[...]), mask_token[...])
        scaled, _ = normalize(rows + placed[at, :].astype(full_type))
        cot[at, :] = (scaled * decoder_gain[...] + decoder_bias[...]).astype(half_type)

    stores = []

    def store(k, source, target):
        copy = pltpu.make_async_copy(source, target, load_sems.at[k])
        copy.start()
        stores.append(copy)

    def feature_part(k):
        if k == 0:
            each_block(patches // 64, 64, decoder_place)
            store(0, cot, decoded_out)
        if k == 1:
            column_blocks(width // WIDE, feature_columns)
        if k == 2:
            scatter[...] = gather[...].T
            each_block(batch // 32, 32, feature_rows)
            row_blocks(patches // 128, 128, feature_place)
            store(1, feats, feature_out)

    def products(t, n, which, put):
        part = nn_dot(turned[t][which, n % 2], rhs_cat[t][n // 2])
        for z in range(z_count):
            for h in range(2):
                put(
                    h,
                    z,
                    part[z * piece : (z + 1) * piece, h * LANES : (h + 1) * LANES],
                )

    def stage0(t, n):
        def put_send(h, z, value):
            core_send[t][n % 2, h, z] = value.astype(half_type)

        def put_own(h, z, value):
            acc[t][n, h, z] = value

        j = n // 2
        if n == 0:
            for i in range(1 if t == 0 else inner // group):
                copies["e", t, i].wait()
        if n % 2 == 0:
            if t == 1:
                for h in range(2):
                    first = pl.multiple_of(h * half + j * LANES, LANES)
                    rhs_cat_b[j, 0:batch, h * LANES : (h + 1) * LANES] = grad_encoded[
                        :, pl.ds(first, LANES)
                    ]
            for h in range(2):
                copies["l", t, j, h].wait()
        products(t, n, 1 - core, put_send)
        send(
            ("c", t, n), core_send[t].at[n % 2], core_land[t].at[n], pair_sems, (0, t, n), sibling
        )
        products(t, n, core, put_own)

    def stage1(t, n):
        r = kept[t]
        copies["c", t, n].wait()
        half_send[t][n % RING] = (
            acc[t][n, 1 - r] + core_land[t][n, 1 - r].astype(full_type)
        ).astype(half_type)
        send(
            ("h", t, n),
            half_send[t].at[n % RING],
            half_land[t].at[n],
            pair_sems,
            (1, t, n),
            half_peer[t],
        )
        acc[t][n, r] = acc[t][n, r] + core_land[t][n, r].astype(full_type)

    def stage2(t, n):
        r = kept[t]
        copies["h", t, n].wait()
        for e in range(2):
            z = 2 * e + 1 - z_low
            near_send[t][n % RING, e] = (
                acc[t][n, r, z] + half_land[t][n, z].astype(full_type)
            ).astype(half_type)
        send(
            ("n", t, n), near_send[t].at[n % RING], near_land[t].at[n], pair_sems, (2, t, n), near_z
        )
        for e in range(2):
            z = 2 * e + z_low
            acc[t][n, r, z] = acc[t][n, r, z] + half_land[t][n, z].astype(full_type)

    def stage3(t, n):
        r = kept[t]
        copies["n", t, n].wait()
        z = z_low + 2 * (1 - z_high)
        far_send[t][n % FAR_RING] = (
            acc[t][n, r, z] + near_land[t][n, 1 - z_high].astype(full_type)
        ).astype(half_type)
        send(("f", t, n), far_send[t].at[n % FAR_RING], far_land[t].at[n], pair_sems, (3, t, n), far_z)
        acc[t][n, r, my_z] = acc[t][n, r, my_z] + near_land[t][n, z_high].astype(full_type)

    def stage4(t, n):
        copies["f", t, n].wait()
        mine = 2 * x + y
        gathered[t][mine, n] = (
            acc[t][n, kept[t], my_z] + far_land[t][n].astype(full_type)
        ).astype(half_type)
        ways = (across_x, across_y, diagonal) if n >= relayed else (across_x, across_y)
        for k, peer in enumerate(ways):
            send(
                ("s", t, n, k),
                gathered[t].at[mine, n],
                gathered[t].at[mine, n],
                spread_sems,
                (t, n, k),
                peer,
            )

    def stage5(t, n):
        for k in range(2):
            copies["s", t, n, k].wait()
        if n >= relayed:
            return
        owner, peer = ((2 * x + 1 - y, across_x), (2 * (1 - x) + y, across_y))[n % 4 == 0]
        passed = gathered[t].at[owner, n]
        send(("s", t, n, 2), passed, passed, spread_sems, (t, n, 2), peer)

    def stage6(t, n):
        copies["s", t, n, 2].wait()
        copy = pltpu.make_async_copy(
            gathered[t].at[:, n], (out_a, out_b)[t].at[:, n], out_sems.at[t, n]
        )
        copy.start()
        stores.append(copy)

    feature_part(1)
    feature_part(2)
    feature_part(0)
    items = [(t, n) for n in range(2 * chunks) for t in (0, 1)]
    stages = (
        (stage6, 22),
        (stage5, 18),
        (stage4, 14),
        (stage3, 10),
        (stage2, 6),
        (stage1, 2),
        (stage0, 0),
    )
    for step in range(len(items) + 22):
        if step < len(items):
            t, n = items[step]
            if n % 2 == 0 and n // 2 + ahead < chunks:
                late(t, n // 2 + ahead)
        for stage, lag in stages:
            i = step - lag
            if 0 <= i < len(items):
                stage(*items[i])
    for copy in stores:
        copy.wait()


def fused(row_data, upstream_rows, visible, positions, matrices, vectors, tiles):
    patches, width = row_data.shape
    fc1_weight, fc2_weight, embed_weight, position_table = matrices
    inner, dec_width = fc1_weight.shape[1], embed_weight.shape[1]
    rows = patches // 2
    z_count = tiles // 2
    block = width // tiles
    piece = block // 2
    chunks = width // 2 // LANES
    whole = pl.BlockSpec(memory_space=pltpu.VMEM)
    away = pl.BlockSpec(memory_space=pl.ANY)
    half, full = jnp.bfloat16, jnp.float32
    shapes = [
        ((16, inner), full),
        ((patches, width), half),
        ((patches, dec_width), half),
        (fc1_weight.shape, half),
        (fc2_weight.shape, half),
        (embed_weight.shape, half),
        (position_table.shape, half),
        ((rows, patches), half),
        ((patches, rows), half),
        ((rows, width), half),
        ((rows, width), full),
        ((rows, 1), full),
        ((rows, width), half),
        ((rows, inner), half),
        ((rows, inner), full),
        ((2, 2, 2, z_count * piece, rows), half),
        ((rows, width), full),
        ((rows, 1), full),
        ((rows, width), half),
        ((rows, dec_width), half),
        ((patches, dec_width), half),
        ((rows, dec_width), half),
        ((rows, dec_width), half),
        ((rows, dec_width), half),
        ((rows, width), full),
        ((rows, width), half),
        ((rows, inner), half),
    ]
    for lead, kind in (
        ((2, 2, z_count * piece, 2 * rows), half),
        ((chunks, 2 * rows, 2 * LANES), half),
        ((4, 2 * chunks, piece, LANES), half),
        ((2 * chunks, 2, z_count, piece, LANES), full),
        ((2, 2, z_count, piece, LANES), half),
        ((2 * chunks, 2, z_count, piece, LANES), half),
        ((RING, z_count, piece, LANES), half),
        ((2 * chunks, z_count, piece, LANES), half),
        ((RING, 2, piece, LANES), half),
        ((2 * chunks, 2, piece, LANES), half),
        ((FAR_RING, piece, LANES), half),
        ((2 * chunks, piece, LANES), half),
    ):
        shapes += [(lead, kind)] * 2
    scratch = [pltpu.VMEM(lead, kind) for lead, kind in shapes]
    scratch += [
        pltpu.SemaphoreType.DMA((7,)),
        pltpu.SemaphoreType.DMA((2, 2, 2)),
        pltpu.SemaphoreType.DMA((2, 2, chunks, 2)),
        pltpu.SemaphoreType.DMA((2, 4, 2, 2 * chunks)),
        pltpu.SemaphoreType.DMA((2, 2, 2 * chunks, 3)),
        pltpu.SemaphoreType.DMA((2, 2 * chunks)),
    ]
    return pl.pallas_call(
        functools.partial(fused_kernel, chunks, z_count),
        out_shape=(
            jax.ShapeDtypeStruct((4, 2 * chunks, piece, LANES), half),
            jax.ShapeDtypeStruct((4, 2 * chunks, piece, LANES), half),
            jax.ShapeDtypeStruct((patches, width), half),
            jax.ShapeDtypeStruct((patches, dec_width), half),
        ),
        in_specs=[whole] * 12 + [away] * 6,
        out_specs=(away,) * 4,
        scratch_shapes=scratch,
        compiler_params=pltpu.CompilerParams(
            collective_id=0, has_side_effects=True, vmem_limit_bytes=60 * 2**20
        ),
    )(
        visible.reshape(1, patches),
        positions.reshape(1, patches),
        *vectors,
        row_data,
        upstream_rows,
        fc1_weight,
        fc2_weight,
        embed_weight,
        position_table,
    )


def finish_kernel(
    count,
    part_a,
    part_b,
    features,
    decoded,
    full_a,
    full_b,
    feature_out,
    decoded_out,
    held_a,
    held_b,
    held_features,
    held_decoded,
    wide_a,
    wide_b,
    read_sems,
    write_sems,
):
    reads = []
    for k, (source, held) in enumerate(
        (
            (features, held_features),
            (part_a, held_a),
            (part_b, held_b),
            (decoded, held_decoded),
        )
    ):
        reads.append(pltpu.make_async_copy(source, held, read_sems.at[k]))
        reads[-1].start()
    writes = []
    for k, (held, wide, target) in enumerate(
        (
            (held_features, held_features, feature_out),
            (held_a, wide_a, full_a),
            (held_b, wide_b, full_b),
            (held_decoded, held_decoded, decoded_out),
        )
    ):
        reads[k].wait()
        if k in (1, 2):
            pieces, piece = held.shape[1], held.shape[2]
            for mine in range(4):
                for n in range(pieces):
                    value = held[mine, n].astype(jnp.float32) / count
                    low, at = (n % 2) * piece, (n // 2) * LANES
                    if k == 1:
                        at += mine * (pieces // 2) * LANES
                    else:
                        low += (mine % 2) * 2 * piece
                        at += (mine // 2) * (pieces // 2) * LANES
                    wide[low : low + piece, at : at + LANES] = value
        writes.append(pltpu.make_async_copy(wide, target, write_sems.at[k]))
        writes[-1].start()
    for write in writes:
        write.wait()


def finish(part_a, part_b, features, decoded, count):
    away = pl.BlockSpec(memory_space=pltpu.HBM)
    _, pieces, piece, _ = part_a.shape
    shapes = ((2 * piece, 2 * pieces * LANES), (4 * piece, pieces * LANES))
    full = jnp.float32
    return pl.pallas_call(
        functools.partial(finish_kernel, float(count)),
        out_shape=(
            jax.ShapeDtypeStruct(shapes[0], full),
            jax.ShapeDtypeStruct(shapes[1], full),
            jax.ShapeDtypeStruct(features.shape, features.dtype),
            jax.ShapeDtypeStruct(decoded.shape, decoded.dtype),
        ),
        in_specs=[away] * 4,
        out_specs=(away,) * 4,
        scratch_shapes=[
            pltpu.VMEM(part.shape, part.dtype) for part in (part_a, part_b, features, decoded)
        ]
        + [pltpu.VMEM(shape, full) for shape in shapes]
        + [pltpu.SemaphoreType.DMA((4,))] * 2,
        compiler_params=pltpu.CompilerParams(vmem_limit_bytes=60 * 2**20),
    )(part_a, part_b, features, decoded)


def reducible(patches, width, inner, dec_width, scenes, tiles):
    return (
        scenes == 4
        and tiles == 8
        and inner == 2 * width
        and width % (tiles * 16) == 0
        and width % WIDE == 0
        and (width // tiles * 8) % WIDE == 0
        and inner % (width // tiles * 8) == 0
        and inner // (width // tiles * 8) == 2
        and patches % 256 == 0
        and width // tiles == 160
        and dec_width % (4 * LANES) == 0
    )


def shards(
    features,
    visible,
    positions,
    cotangent,
    mlp_gain,
    mlp_bias,
    fc1_weight,
    fc1_bias,
    fc2_weight,
    fc2_bias,
    encoder_gain,
    encoder_bias,
    embed_weight,
    embed_bias,
    mask_token,
    position_table,
    decoder_gain,
    decoder_bias,
):
    patch_count = features.shape[2]
    model_width = features.shape[3]
    dec_width = embed_weight.shape[1]
    tiles = lax.axis_size("tile")
    scenes = lax.axis_size("dp")
    most_rows = patch_count // 2
    flags = visible.reshape(patch_count)
    row_data = features.reshape(patch_count, model_width)
    if reducible(
        patch_count, model_width, fc1_weight.shape[1], dec_width, scenes, tiles
    ):
        total_a, total_b, grad_rows, decoded = fused(
            row_data,
            cotangent.reshape(patch_count, dec_width),
            visible,
            positions,
            (fc1_weight, fc2_weight, embed_weight, position_table),
            (
                mlp_gain,
                mlp_bias,
                fc1_bias,
                fc2_bias,
                encoder_gain,
                encoder_bias,
                embed_bias,
                mask_token,
                decoder_gain,
                decoder_bias,
            ),
            tiles,
        )
        fc1_grad, fc2_grad, grad_rows, decoded = finish(
            total_a, total_b, grad_rows, decoded, scenes * tiles
        )
        return (
            grad_rows.reshape(features.shape),
            decoded.reshape(cotangent.shape),
            fc1_grad,
            fc2_grad,
        )
    keep_rows = (flags > 0)[:, None]
    upstream = cotangent.reshape(patch_count, dec_width)
    ids = jnp.arange(patch_count, dtype=jnp.int32)
    row_rank = jnp.sum(jnp.where(ids[None, :] < ids[:, None], flags[None, :], 0), axis=1)
    slots = jnp.arange(most_rows, dtype=jnp.int32)
    target = jnp.where(flags > 0, row_rank, -1)
    gather = (slots[:, None] == target[None, :]).astype(jnp.bfloat16)
    scatter = (target[:, None] == slots[None, :]).astype(jnp.bfloat16)
    enc_params = (
        mlp_gain,
        mlp_bias,
        fc1_weight,
        fc1_bias,
        fc2_weight,
        fc2_bias,
        encoder_gain,
        encoder_bias,
        embed_weight,
        embed_bias,
    )
    decoder_args = (position_table, mask_token, decoder_gain, decoder_bias)
    enc_input = jnp.dot(gather, row_data, preferred_element_type=jnp.bfloat16)
    saved, projected = encode(enc_input, enc_params)
    projected_rows = jnp.dot(scatter, projected, preferred_element_type=jnp.float32)
    decoded, grad_projected = decoder_pass(
        projected_rows, keep_rows, positions.reshape(-1), upstream, *decoder_args
    )
    grad_compact = jnp.dot(gather, grad_projected, preferred_element_type=jnp.bfloat16)
    mlp_in, grad_pre, hidden, grad_encoded, grad_feats = encode_back(
        saved, grad_compact, enc_params
    )
    device_total = scenes * tiles
    grad_rows = jnp.dot(scatter, grad_feats, preferred_element_type=jnp.bfloat16)
    totals = []
    for left, right in ((mlp_in, grad_pre), (hidden, grad_encoded)):
        term = jnp.dot(left.T, right, preferred_element_type=jnp.float32)
        share = lax.psum_scatter(
            term.astype(jnp.bfloat16), "tile", scatter_dimension=0, tiled=True
        )
        totals.append(lax.psum(share, "dp").astype(jnp.float32))
    fc1_grad, fc2_grad = [total / device_total for total in totals]
    feature_grad = grad_rows.reshape(features.shape)
    decoded_out = decoded.reshape(cotangent.shape)
    return (feature_grad, decoded_out, fc1_grad, fc2_grad)


def solution(mesh):
    return jax.shard_map(
        shards,
        mesh=mesh,
        in_specs=(
            P("dp", "tile", None, None),
            P("dp", "tile", None),
            P("dp", "tile", None),
            P("dp", "tile", None, None),
            P(),
            P(),
            P(),
            P(),
            P(),
            P(),
            P(),
            P(),
            P(),
            P(),
            P(),
            P(),
            P(),
            P(),
        ),
        out_specs=(
            P("dp", "tile", None, None),
            P("dp", "tile", None, None),
            P("tile", None),
            P("tile", None),
        ),
        check_vma=False,
    )
```

```python
import functools

import jax
import jax.numpy as jnp
from jax import lax
from jax.experimental import pallas as pl
from jax.experimental.pallas import tpu as pltpu
from jax.sharding import PartitionSpec as P

MESH = pl.DeviceIdType.MESH

epsilon = 1e-06


def layer_norm(values, norm_gain, norm_bias):
    row_mean = jnp.mean(values, axis=-1, keepdims=True)
    centred = values - row_mean
    variance = jnp.mean(centred * centred, axis=-1, keepdims=True)
    inv_std = lax.rsqrt(variance + epsilon)
    scaled = centred * inv_std
    return (scaled * norm_gain + norm_bias, scaled, inv_std)


def norm_back(upstream, scaled, inv_std):
    mean_up = jnp.mean(upstream, axis=-1, keepdims=True)
    mean_cross = jnp.mean(upstream * scaled, axis=-1, keepdims=True)
    return inv_std * (upstream - mean_up - scaled * mean_cross)


def gelu_parts(pre_act):
    normal_cdf = 0.5 * (1.0 + lax.erf(pre_act * 0.7071067811865476))
    density = jnp.exp(-0.5 * pre_act * pre_act) * 0.3989422804014327
    return (pre_act * normal_cdf, normal_cdf + pre_act * density)


def encode(enc_input, enc_params):
    (
        mlp_gain,
        mlp_bias,
        fc1_weight,
        fc1_bias,
        fc2_weight,
        fc2_bias,
        encoder_gain,
        encoder_bias,
        embed_weight,
        embed_bias,
    ) = enc_params
    rows_in = enc_input.astype(jnp.float32)
    mlp_in, mlp_scaled, mlp_inv = layer_norm(rows_in, mlp_gain, mlp_bias)
    mlp_in = mlp_in.astype(jnp.bfloat16)
    pre_act = jnp.dot(mlp_in, fc1_weight, preferred_element_type=jnp.float32) + fc1_bias
    activation, slope = gelu_parts(pre_act)
    hidden = activation.astype(jnp.bfloat16)
    encoded = rows_in + jnp.dot(hidden, fc2_weight, preferred_element_type=jnp.float32) + fc2_bias
    normed, enc_scaled, enc_inv = layer_norm(encoded, encoder_gain, encoder_bias)
    normed = normed.astype(jnp.bfloat16)
    projected = (
        jnp.dot(normed, embed_weight, preferred_element_type=jnp.float32) + embed_bias
    ).astype(jnp.bfloat16)
    saved = (mlp_in, mlp_scaled, mlp_inv, slope, hidden, enc_scaled, enc_inv)
    return (saved, projected)


def encode_back(saved, grad_compact, enc_params):
    (
        mlp_gain,
        mlp_bias,
        fc1_weight,
        fc1_bias,
        fc2_weight,
        fc2_bias,
        encoder_gain,
        encoder_bias,
        embed_weight,
        embed_bias,
    ) = enc_params
    mlp_in, mlp_scaled, mlp_inv, slope, hidden, enc_scaled, enc_inv = saved
    grad_normed = jnp.dot(grad_compact, embed_weight.T, preferred_element_type=jnp.float32)
    grad_encoded = norm_back(grad_normed * encoder_gain, enc_scaled, enc_inv).astype(jnp.bfloat16)
    grad_hidden = jnp.dot(grad_encoded, fc2_weight.T, preferred_element_type=jnp.float32)
    grad_pre = (grad_hidden * slope).astype(jnp.bfloat16)
    grad_mlp_in = jnp.dot(grad_pre, fc1_weight.T, preferred_element_type=jnp.float32)
    grad_feats = (
        grad_encoded.astype(jnp.float32) + norm_back(grad_mlp_in * mlp_gain, mlp_scaled, mlp_inv)
    ).astype(jnp.bfloat16)
    return (mlp_in, grad_pre, hidden, grad_encoded, grad_feats)


def decoder_pass(
    projected_rows,
    keep_rows,
    position_ids,
    upstream,
    position_table,
    mask_token,
    decoder_gain,
    decoder_bias,
):
    table_ids = jnp.arange(position_table.shape[0], dtype=jnp.int32)[None, :]
    pick = (position_ids[:, None] == table_ids).astype(jnp.bfloat16)
    placed = jnp.dot(pick, position_table, preferred_element_type=jnp.float32)
    dec_input = jnp.where(keep_rows, projected_rows, mask_token) + placed
    decoded, dec_scaled, dec_inv = layer_norm(dec_input, decoder_gain, decoder_bias)
    grad_input = norm_back(upstream.astype(jnp.float32) * decoder_gain, dec_scaled, dec_inv)
    grad_projected = jnp.where(keep_rows, grad_input, 0.0).astype(jnp.bfloat16)
    return (decoded.astype(jnp.bfloat16), grad_projected)


LANES = 128
WIDE = 256
RING = 3
FAR_RING = 6


def normalize(values):
    row_mean = jnp.mean(values, axis=-1, keepdims=True)
    centred = values - row_mean
    variance = jnp.mean(centred * centred, axis=-1, keepdims=True)
    inv_std = lax.rsqrt(variance + epsilon)
    return (centred * inv_std, inv_std)


def nt_dot(left, right):
    return lax.dot_general(
        left, right, (((1,), (1,)), ((), ())), preferred_element_type=jnp.float32
    )


def nn_dot(left, right):
    return jnp.dot(left, right, preferred_element_type=jnp.float32)


def fused_kernel(
    chunks,
    z_count,
    visible,
    positions,
    mlp_gain,
    mlp_bias,
    fc1_bias,
    fc2_bias,
    encoder_gain,
    encoder_bias,
    embed_bias,
    mask_token,
    decoder_gain,
    decoder_bias,
    features,
    cotangent,
    fc1_weight,
    fc2_weight,
    embed_weight,
    position_table,
    out_a,
    out_b,
    feature_out,
    decoded_out,
    vectors,
    feats,
    cot,
    fc1,
    fc2,
    embed,
    table,
    gather,
    scatter,
    rows_in,
    mlp_scaled,
    mlp_inv,
    mlp_in,
    hidden,
    slope,
    by_half,
    encoded,
    enc_inv,
    normed,
    projected,
    placed,
    placed_rows,
    cot_rows,
    grad_rows,
    upstream,
    grad_encoded,
    grad_pre,
    turned_a,
    turned_b,
    rhs_cat_a,
    rhs_cat_b,
    gathered_a,
    gathered_b,
    acc_a,
    acc_b,
    core_send_a,
    core_send_b,
    core_land_a,
    core_land_b,
    half_send_a,
    half_send_b,
    half_land_a,
    half_land_b,
    near_send_a,
    near_send_b,
    near_land_a,
    near_land_b,
    far_send_a,
    far_send_b,
    far_land_a,
    far_land_b,
    load_sems,
    early_sems,
    late_sems,
    pair_sems,
    spread_sems,
    out_sems,
):
    half_type, full_type = jnp.bfloat16, jnp.float32
    for row, vector in enumerate(
        (
            mlp_gain,
            mlp_bias,
            fc1_bias,
            fc2_bias,
            encoder_gain,
            encoder_bias,
            embed_bias,
            mask_token,
            decoder_gain,
            decoder_bias,
        )
    ):
        vectors[row : row + 1, 0 : vector.shape[0]] = vector[...].reshape(1, -1)
    (
        mlp_gain,
        mlp_bias,
        fc1_bias,
        fc2_bias,
        encoder_gain,
        encoder_bias,
        embed_bias,
        mask_token,
        decoder_gain,
        decoder_bias,
    ) = [
        vectors.at[row : row + 1, 0 : vector.shape[0]]
        for row, vector in enumerate(
            (
                mlp_gain,
                mlp_bias,
                fc1_bias,
                fc2_bias,
                encoder_gain,
                encoder_bias,
                embed_bias,
                mask_token,
                decoder_gain,
                decoder_bias,
            )
        )
    ]
    dp = lax.axis_index("dp")
    tile = lax.axis_index("tile")
    x = lax.rem(dp, 2)
    y = lax.div(dp, 2)
    core = lax.rem(tile, 2)
    my_z = lax.div(tile, 2)
    sibling = (dp, tile + 1 - 2 * core)
    across_x = (dp + 1 - 2 * x, tile)
    across_y = (dp + 2 - 4 * y, tile)
    diagonal = (3 - dp, tile)
    z_low, z_high = lax.rem(my_z, 2), lax.div(my_z, 2)
    near_z = (dp, tile + 2 - 4 * z_low)
    far_z = (dp, tile + 4 - 8 * z_high)
    peers = [sibling, across_x, across_y, diagonal, near_z, far_z]

    barrier = pltpu.get_barrier_semaphore()
    for peer in peers:
        pl.semaphore_signal(barrier, inc=1, device_id=peer, device_id_type=MESH)
    halves = fc1.shape[1] // 2
    load_feats = pltpu.make_async_copy(features, feats, load_sems.at[0])
    load_fc1 = [
        pltpu.make_async_copy(
            fc1_weight.at[:, k * halves : (k + 1) * halves],
            fc1.at[:, k * halves : (k + 1) * halves],
            load_sems.at[1 + k],
        )
        for k in range(2)
    ]
    load_table = pltpu.make_async_copy(position_table, table, load_sems.at[3])
    load_cot = pltpu.make_async_copy(cotangent, cot, load_sems.at[4])
    load_embed = pltpu.make_async_copy(embed_weight, embed, load_sems.at[5])
    load_fc2 = pltpu.make_async_copy(fc2_weight, fc2, load_sems.at[6])
    for load in (load_feats, load_fc1[0], load_table, load_cot):
        load.start()

    patches, width = feats.shape
    batch, inner = hidden.shape
    piece = turned_a.shape[2] // z_count
    block = 2 * piece
    half = chunks * LANES
    turned = (turned_a, turned_b)
    rhs = (grad_pre, grad_encoded)
    rhs_cat = (rhs_cat_a, rhs_cat_b)
    gathered = (gathered_a, gathered_b)
    acc = (acc_a, acc_b)
    core_send, core_land = (core_send_a, core_send_b), (core_land_a, core_land_b)
    half_send, half_land = (half_send_a, half_send_b), (half_land_a, half_land_b)
    near_send, near_land = (near_send_a, near_send_b), (near_land_a, near_land_b)
    far_send, far_land = (far_send_a, far_send_b), (far_land_a, far_land_b)
    gather_peer = (across_x, across_y)
    half_peer = (across_y, across_x)
    kept = (y, x)
    own_base = (x * 2 * half, 0)
    far_base = ((1 - x) * 2 * half, 0)
    copies = {}

    def send(key, src, dst, sems, at, peer):
        copy = pltpu.make_async_remote_copy(
            src_ref=src,
            dst_ref=dst,
            send_sem=sems.at[(0,) + at],
            recv_sem=sems.at[(1,) + at],
            device_id=peer,
            device_id_type=MESH,
        )
        copy.start()
        copies[key] = copy

    def row_blocks(count, tall, body):
        @pl.loop(0, count)
        def _(i):
            body(pl.ds(pl.multiple_of(i * tall, tall), tall))

    def each_block(count, tall, body):
        for i in range(count):
            body(slice(i * tall, (i + 1) * tall))

    def column_blocks(count, body):
        @pl.loop(0, count)
        def _(i):
            body(pl.ds(pl.multiple_of(i * WIDE, WIDE), WIDE))

    flags = visible[...] > 0
    ones = jnp.broadcast_to(jnp.where(flags, 1.0, 0.0), (16, patches)).astype(half_type)
    before = lax.broadcasted_iota(jnp.int32, (patches, patches), 0) < lax.broadcasted_iota(
        jnp.int32, (patches, patches), 1
    )
    rank = nn_dot(ones, jnp.where(before, 1.0, 0.0).astype(half_type))[0:1, :]
    target = jnp.where(flags, rank, -1.0).astype(jnp.int32)
    slot = lax.broadcasted_iota(jnp.int32, (batch, patches), 0)
    gather[...] = jnp.where(slot == target, 1.0, 0.0).astype(half_type)
    load_feats.wait()
    load_fc1[1].start()

    def compact(at):
        rows_in[:, at] = nn_dot(gather[...], feats[:, at]).astype(half_type)

    each_block(width // WIDE, WIDE, compact)

    def first_norm(at):
        scaled, inverse = normalize(rows_in[at, :].astype(full_type))
        mlp_scaled[at, :] = scaled
        mlp_inv[at, :] = inverse
        mlp_in[at, :] = (scaled * mlp_gain[...] + mlp_bias[...]).astype(half_type)

    each_block(batch // 32, 32, first_norm)
    for at in range(0, width, WIDE):
        flipped = mlp_in[:, at : at + WIDE].T
        row = at
        while row < at + WIDE:
            number, upper = row // block, row // piece
            stop = min(at + WIDE, (upper + 1) * piece)
            first = (number // 2) * piece + row - upper * piece
            turned_a[number % 2, upper % 2, first : first + stop - row, 0:batch] = flipped[
                row - at : stop - at
            ]
            row = stop
    pl.semaphore_wait(barrier, len(peers))
    send(
        ("e", 0, 0),
        turned_a.at[:, :, :, 0:batch],
        turned_a.at[:, :, :, batch : 2 * batch],
        early_sems,
        (0, 0),
        across_x,
    )

    load_fc2.start()
    load_embed.start()
    group = 8 * block
    for i in range(inner // group):
        load_fc1[i].wait()
        for at in range(0, group, WIDE):
            columns = slice(i * group + at, i * group + at + WIDE)
            pre_act = nn_dot(mlp_in[...], fc1[:, columns]) + fc1_bias[:, columns]
            activation, slope[:, columns] = gelu_parts(pre_act)
            activation = activation.astype(half_type)
            hidden[:, columns] = activation
            flipped = activation.T
            row = at
            while row < at + WIDE:
                number, upper = row // block, row // piece
                stop = min(at + WIDE, (upper + 1) * piece)
                first = (2 * i + number // 4) * piece + row - upper * piece
                by_half[
                    number % 2, (number // 2) % 2, upper % 2, first : first + stop - row, :
                ] = flipped[row - at : stop - at]
                row = stop
        part = slice(2 * i * piece, 2 * (i + 1) * piece)
        send(
            ("e", 1, i),
            by_half.at[1 - y, :, :, part, :],
            turned_b.at[:, :, part, batch : 2 * batch],
            early_sems,
            (1, i),
            across_y,
        )
    turned_b[:, :, :, 0:batch] = by_half[y]
    load_table.wait()
    load_cot.wait()
    names = lax.broadcasted_iota(jnp.int32, (patches, patches), 0)
    pick = jnp.where(names == positions[...], 1.0, 0.0).astype(half_type).T
    placed[...] = nn_dot(pick, table[...]).astype(half_type)
    placed_rows[...] = nn_dot(gather[...], placed[...]).astype(half_type)
    cot_rows[...] = nn_dot(gather[...], cot[...]).astype(half_type)

    load_fc2.wait()

    def second_product(at):
        encoded[:, at] = (
            rows_in[:, at].astype(full_type) + nn_dot(hidden[...], fc2[:, at]) + fc2_bias[:, at]
        )

    column_blocks(width // WIDE, second_product)

    def second_norm(at):
        scaled, inverse = normalize(encoded[at, :])
        encoded[at, :] = scaled
        enc_inv[at, :] = inverse
        normed[at, :] = (scaled * encoder_gain[...] + encoder_bias[...]).astype(half_type)

    each_block(batch // 32, 32, second_norm)
    load_embed.wait()
    projected[...] = (nn_dot(normed[...], embed[...]) + embed_bias[...]).astype(half_type)

    def decoder_rows(at):
        scaled, inverse = normalize(
            projected[at, :].astype(full_type) + placed_rows[at, :].astype(full_type)
        )
        back = norm_back(cot_rows[at, :].astype(full_type) * decoder_gain[...], scaled, inverse)
        grad_rows[at, :] = back.astype(half_type)

    each_block(batch // 32, 32, decoder_rows)

    def embed_back(at):
        upstream[:, at] = nt_dot(grad_rows[...], embed[at, :]) * encoder_gain[:, at]

    each_block(width // WIDE, WIDE, embed_back)

    def encoder_back(at):
        grad_encoded[at, :] = norm_back(upstream[at, :], encoded[at, :], enc_inv[at, :]).astype(
            half_type
        )

    each_block(batch // 32, 32, encoder_back)

    def late(t, j):
        for h in range(2):
            first = pl.multiple_of(far_base[t] + h * half + j * LANES, LANES)
            send(
                ("l", t, j, h),
                rhs[t].at[:, pl.ds(first, LANES)],
                rhs_cat[t].at[j, batch : 2 * batch, h * LANES : (h + 1) * LANES],
                late_sems,
                (t, j, h),
                gather_peer[t],
            )

    def pre_columns(base, j, own):
        at = [
            pl.ds(pl.multiple_of(base + h * half + j * LANES, LANES), LANES) for h in range(2)
        ]
        weights = jnp.concatenate([fc2[at[0], :], fc2[at[1], :]], axis=0)
        part = nt_dot(grad_encoded[...], weights)
        for h in range(2):
            value = (part[:, h * LANES : (h + 1) * LANES] * slope[:, at[h]]).astype(half_type)
            grad_pre[:, at[h]] = value
            if own:
                rhs_cat_a[j, 0:batch, h * LANES : (h + 1) * LANES] = value

    ahead = 1
    relayed = 2 * chunks - 2
    for j in range(ahead):
        late(1, j)
    for j in range(chunks):
        pre_columns(far_base[0], j, False)
        if j < ahead:
            late(0, j)
    for j in range(chunks):
        pre_columns(own_base[0], j, True)

    def feature_columns(at):
        upstream[:, at] = nt_dot(grad_pre[...], fc1[at, :]) * mlp_gain[:, at]

    def feature_rows(at):
        back = norm_back(upstream[at, :], mlp_scaled[at, :], mlp_inv[at, :])
        normed[at, :] = (grad_encoded[at, :].astype(full_type) + back).astype(half_type)

    def feature_place(at):
        feats[at, :] = nn_dot(scatter[at, :], normed[...]).astype(half_type)

    def decoder_place(at):
        picks = scatter[at, :]
        keep_rows = jnp.sum(picks.astype(full_type), axis=1, keepdims=True) > 0.5
        rows = jnp.where(keep_rows, nn_dot(picks, projected[...]), mask_token[...])
        scaled, _ = normalize(rows + placed[at, :].astype(full_type))
        cot[at, :] = (scaled * decoder_gain[...] + decoder_bias[...]).astype(half_type)

    stores = []

    def store(k, source, target):
        copy = pltpu.make_async_copy(source, target, load_sems.at[k])
        copy.start()
        stores.append(copy)

    def feature_part(k):
        if k == 0:
            each_block(patches // 64, 64, decoder_place)
            store(0, cot, decoded_out)
        if k == 1:
            column_blocks(width // WIDE, feature_columns)
        if k == 2:
            scatter[...] = gather[...].T
            each_block(batch // 32, 32, feature_rows)
            row_blocks(patches // 128, 128, feature_place)
            store(1, feats, feature_out)

    def products(t, n, which, put):
        part = nn_dot(turned[t][which, n % 2], rhs_cat[t][n // 2])
        for z in range(z_count):
            for h in range(2):
                put(
                    h,
                    z,
                    part[z * piece : (z + 1) * piece, h * LANES : (h + 1) * LANES],
                )

    def stage0(t, n):
        def put_send(h, z, value):
            core_send[t][n % 2, h, z] = value.astype(half_type)

        def put_own(h, z, value):
            acc[t][n, h, z] = value

        j = n // 2
        if n == 0:
            for i in range(1 if t == 0 else inner // group):
                copies["e", t, i].wait()
        if n % 2 == 0:
            if t == 1:
                for h in range(2):
                    first = pl.multiple_of(h * half + j * LANES, LANES)
                    rhs_cat_b[j, 0:batch, h * LANES : (h + 1) * LANES] = grad_encoded[
                        :, pl.ds(first, LANES)
                    ]
            for h in range(2):
                copies["l", t, j, h].wait()
        products(t, n, 1 - core, put_send)
        send(
            ("c", t, n), core_send[t].at[n % 2], core_land[t].at[n], pair_sems, (0, t, n), sibling
        )
        products(t, n, core, put_own)

    def stage1(t, n):
        r = kept[t]
        copies["c", t, n].wait()
        half_send[t][n % RING] = (
            acc[t][n, 1 - r] + core_land[t][n, 1 - r].astype(full_type)
        ).astype(half_type)
        send(
            ("h", t, n),
            half_send[t].at[n % RING],
            half_land[t].at[n],
            pair_sems,
            (1, t, n),
            half_peer[t],
        )
        acc[t][n, r] = acc[t][n, r] + core_land[t][n, r].astype(full_type)

    def stage2(t, n):
        r = kept[t]
        copies["h", t, n].wait()
        for e in range(2):
            z = 2 * e + 1 - z_low
            near_send[t][n % RING, e] = (
                acc[t][n, r, z] + half_land[t][n, z].astype(full_type)
            ).astype(half_type)
        send(
            ("n", t, n), near_send[t].at[n % RING], near_land[t].at[n], pair_sems, (2, t, n), near_z
        )
        for e in range(2):
            z = 2 * e + z_low
            acc[t][n, r, z] = acc[t][n, r, z] + half_land[t][n, z].astype(full_type)

    def stage3(t, n):
        r = kept[t]
        copies["n", t, n].wait()
        z = z_low + 2 * (1 - z_high)
        far_send[t][n % FAR_RING] = (
            acc[t][n, r, z] + near_land[t][n, 1 - z_high].astype(full_type)
        ).astype(half_type)
        send(("f", t, n), far_send[t].at[n % FAR_RING], far_land[t].at[n], pair_sems, (3, t, n), far_z)
        acc[t][n, r, my_z] = acc[t][n, r, my_z] + near_land[t][n, z_high].astype(full_type)

    def stage4(t, n):
        copies["f", t, n].wait()
        mine = 2 * x + y
        gathered[t][mine, n] = (
            acc[t][n, kept[t], my_z] + far_land[t][n].astype(full_type)
        ).astype(half_type)
        ways = (across_x, across_y, diagonal) if n >= relayed else (across_x, across_y)
        for k, peer in enumerate(ways):
            send(
                ("s", t, n, k),
                gathered[t].at[mine, n],
                gathered[t].at[mine, n],
                spread_sems,
                (t, n, k),
                peer,
            )

    def stage5(t, n):
        for k in range(2):
            copies["s", t, n, k].wait()
        if n >= relayed:
            return
        owner, peer = ((2 * x + 1 - y, across_x), (2 * (1 - x) + y, across_y))[n % 4 == 0]
        passed = gathered[t].at[owner, n]
        send(("s", t, n, 2), passed, passed, spread_sems, (t, n, 2), peer)

    def stage6(t, n):
        copies["s", t, n, 2].wait()
        copy = pltpu.make_async_copy(
            gathered[t].at[:, n], (out_a, out_b)[t].at[:, n], out_sems.at[t, n]
        )
        copy.start()
        stores.append(copy)

    feature_part(1)
    feature_part(2)
    feature_part(0)
    items = [(t, n) for n in range(2 * chunks) for t in (0, 1)]
    stages = (
        (stage0, 0),
        (stage1, 2),
        (stage2, 6),
        (stage3, 10),
        (stage4, 14),
        (stage5, 18),
        (stage6, 22),
    )
    for step in range(len(items) + 22):
        if step < len(items):
            t, n = items[step]
            if n % 2 == 0 and n // 2 + ahead < chunks:
                late(t, n // 2 + ahead)
        for stage, lag in stages:
            i = step - lag
            if 0 <= i < len(items):
                stage(*items[i])
    for copy in stores:
        copy.wait()


def fused(row_data, upstream_rows, visible, positions, matrices, vectors, tiles):
    patches, width = row_data.shape
    fc1_weight, fc2_weight, embed_weight, position_table = matrices
    inner, dec_width = fc1_weight.shape[1], embed_weight.shape[1]
    rows = patches // 2
    z_count = tiles // 2
    block = width // tiles
    piece = block // 2
    chunks = width // 2 // LANES
    whole = pl.BlockSpec(memory_space=pltpu.VMEM)
    away = pl.BlockSpec(memory_space=pl.ANY)
    half, full = jnp.bfloat16, jnp.float32
    shapes = [
        ((16, inner), full),
        ((patches, width), half),
        ((patches, dec_width), half),
        (fc1_weight.shape, half),
        (fc2_weight.shape, half),
        (embed_weight.shape, half),
        (position_table.shape, half),
        ((rows, patches), half),
        ((patches, rows), half),
        ((rows, width), half),
        ((rows, width), full),
        ((rows, 1), full),
        ((rows, width), half),
        ((rows, inner), half),
        ((rows, inner), full),
        ((2, 2, 2, z_count * piece, rows), half),
        ((rows, width), full),
        ((rows, 1), full),
        ((rows, width), half),
        ((rows, dec_width), half),
        ((patches, dec_width), half),
        ((rows, dec_width), half),
        ((rows, dec_width), half),
        ((rows, dec_width), half),
        ((rows, width), full),
        ((rows, width), half),
        ((rows, inner), half),
    ]
    for lead, kind in (
        ((2, 2, z_count * piece, 2 * rows), half),
        ((chunks, 2 * rows, 2 * LANES), half),
        ((4, 2 * chunks, piece, LANES), half),
        ((2 * chunks, 2, z_count, piece, LANES), full),
        ((2, 2, z_count, piece, LANES), half),
        ((2 * chunks, 2, z_count, piece, LANES), half),
        ((RING, z_count, piece, LANES), half),
        ((2 * chunks, z_count, piece, LANES), half),
        ((RING, 2, piece, LANES), half),
        ((2 * chunks, 2, piece, LANES), half),
        ((FAR_RING, piece, LANES), half),
        ((2 * chunks, piece, LANES), half),
    ):
        shapes += [(lead, kind)] * 2
    scratch = [pltpu.VMEM(lead, kind) for lead, kind in shapes]
    scratch += [
        pltpu.SemaphoreType.DMA((7,)),
        pltpu.SemaphoreType.DMA((2, 2, 2)),
        pltpu.SemaphoreType.DMA((2, 2, chunks, 2)),
        pltpu.SemaphoreType.DMA((2, 4, 2, 2 * chunks)),
        pltpu.SemaphoreType.DMA((2, 2, 2 * chunks, 3)),
        pltpu.SemaphoreType.DMA((2, 2 * chunks)),
    ]
    return pl.pallas_call(
        functools.partial(fused_kernel, chunks, z_count),
        out_shape=(
            jax.ShapeDtypeStruct((4, 2 * chunks, piece, LANES), half),
            jax.ShapeDtypeStruct((4, 2 * chunks, piece, LANES), half),
            jax.ShapeDtypeStruct((patches, width), half),
            jax.ShapeDtypeStruct((patches, dec_width), half),
        ),
        in_specs=[whole] * 12 + [away] * 6,
        out_specs=(away,) * 4,
        scratch_shapes=scratch,
        compiler_params=pltpu.CompilerParams(
            collective_id=0, has_side_effects=True, vmem_limit_bytes=60 * 2**20
        ),
    )(
        visible.reshape(1, patches),
        positions.reshape(1, patches),
        *vectors,
        row_data,
        upstream_rows,
        fc1_weight,
        fc2_weight,
        embed_weight,
        position_table,
    )


def finish_kernel(
    count,
    part_a,
    part_b,
    features,
    decoded,
    full_a,
    full_b,
    feature_out,
    decoded_out,
    held_a,
    held_b,
    held_features,
    held_decoded,
    wide_a,
    wide_b,
    read_sems,
    write_sems,
):
    pieces, piece = part_a.shape[1], part_a.shape[2]
    wide = pieces // 2 * LANES
    work = []
    for mine in range(4):
        block = full_a.at[:, mine * wide : (mine + 1) * wide]
        inner = wide_a.at[:, mine * wide : (mine + 1) * wide]
        work.append((part_a.at[mine], held_a.at[mine], inner, block))
        at = (
            slice((mine % 2) * 2 * piece, (mine % 2 + 1) * 2 * piece),
            slice((mine // 2) * wide, (mine // 2 + 1) * wide),
        )
        work.append((part_b.at[mine], held_b.at[mine], wide_b.at[at], full_b.at[at]))
        rows = features.shape[0] // 4
        at = slice(mine * rows, (mine + 1) * rows)
        work.append((features.at[at], held_features.at[at], None, feature_out.at[at]))
    work.append((decoded, held_decoded, None, decoded_out))
    reads = []
    for k, (source, held, _, _) in enumerate(work):
        reads.append(pltpu.make_async_copy(source, held, read_sems.at[k]))
        reads[-1].start()
    writes = []
    for k, (_, held, full, target) in enumerate(work):
        reads[k].wait()
        if full is not None:
            for n in range(pieces):
                low, at = (n % 2) * piece, (n // 2) * LANES
                full[low : low + piece, at : at + LANES] = held[n].astype(jnp.float32) / count
        writes.append(
            pltpu.make_async_copy(held if full is None else full, target, write_sems.at[k])
        )
        writes[-1].start()
    for write in writes:
        write.wait()


def finish(part_a, part_b, features, decoded, count):
    away = pl.BlockSpec(memory_space=pltpu.HBM)
    _, pieces, piece, _ = part_a.shape
    shapes = ((2 * piece, 2 * pieces * LANES), (4 * piece, pieces * LANES))
    full = jnp.float32
    return pl.pallas_call(
        functools.partial(finish_kernel, float(count)),
        out_shape=(
            jax.ShapeDtypeStruct(shapes[0], full),
            jax.ShapeDtypeStruct(shapes[1], full),
            jax.ShapeDtypeStruct(features.shape, features.dtype),
            jax.ShapeDtypeStruct(decoded.shape, decoded.dtype),
        ),
        in_specs=[away] * 4,
        out_specs=(away,) * 4,
        scratch_shapes=[
            pltpu.VMEM(part.shape, part.dtype) for part in (part_a, part_b, features, decoded)
        ]
        + [pltpu.VMEM(shape, full) for shape in shapes]
        + [pltpu.SemaphoreType.DMA((13,))] * 2,
        compiler_params=pltpu.CompilerParams(vmem_limit_bytes=60 * 2**20),
    )(part_a, part_b, features, decoded)


def reducible(patches, width, inner, dec_width, scenes, tiles):
    return (
        scenes == 4
        and tiles == 8
        and inner == 2 * width
        and width % (tiles * 16) == 0
        and width % WIDE == 0
        and (width // tiles * 8) % WIDE == 0
        and inner % (width // tiles * 8) == 0
        and inner // (width // tiles * 8) == 2
        and patches % 256 == 0
        and width // tiles == 160
        and dec_width % (4 * LANES) == 0
    )


def shards(
    features,
    visible,
    positions,
    cotangent,
    mlp_gain,
    mlp_bias,
    fc1_weight,
    fc1_bias,
    fc2_weight,
    fc2_bias,
    encoder_gain,
    encoder_bias,
    embed_weight,
    embed_bias,
    mask_token,
    position_table,
    decoder_gain,
    decoder_bias,
):
    patch_count = features.shape[2]
    model_width = features.shape[3]
    dec_width = embed_weight.shape[1]
    tiles = lax.axis_size("tile")
    scenes = lax.axis_size("dp")
    most_rows = patch_count // 2
    flags = visible.reshape(patch_count)
    row_data = features.reshape(patch_count, model_width)
    if reducible(
        patch_count, model_width, fc1_weight.shape[1], dec_width, scenes, tiles
    ):
        total_a, total_b, grad_rows, decoded = fused(
            row_data,
            cotangent.reshape(patch_count, dec_width),
            visible,
            positions,
            (fc1_weight, fc2_weight, embed_weight, position_table),
            (
                mlp_gain,
                mlp_bias,
                fc1_bias,
                fc2_bias,
                encoder_gain,
                encoder_bias,
                embed_bias,
                mask_token,
                decoder_gain,
                decoder_bias,
            ),
            tiles,
        )
        fc1_grad, fc2_grad, grad_rows, decoded = finish(
            total_a, total_b, grad_rows, decoded, scenes * tiles
        )
        return (
            grad_rows.reshape(features.shape),
            decoded.reshape(cotangent.shape),
            fc1_grad,
            fc2_grad,
        )
    keep_rows = (flags > 0)[:, None]
    upstream = cotangent.reshape(patch_count, dec_width)
    ids = jnp.arange(patch_count, dtype=jnp.int32)
    row_rank = jnp.sum(jnp.where(ids[None, :] < ids[:, None], flags[None, :], 0), axis=1)
    slots = jnp.arange(most_rows, dtype=jnp.int32)
    target = jnp.where(flags > 0, row_rank, -1)
    gather = (slots[:, None] == target[None, :]).astype(jnp.bfloat16)
    scatter = (target[:, None] == slots[None, :]).astype(jnp.bfloat16)
    enc_params = (
        mlp_gain,
        mlp_bias,
        fc1_weight,
        fc1_bias,
        fc2_weight,
        fc2_bias,
        encoder_gain,
        encoder_bias,
        embed_weight,
        embed_bias,
    )
    decoder_args = (position_table, mask_token, decoder_gain, decoder_bias)
    enc_input = jnp.dot(gather, row_data, preferred_element_type=jnp.bfloat16)
    saved, projected = encode(enc_input, enc_params)
    projected_rows = jnp.dot(scatter, projected, preferred_element_type=jnp.float32)
    decoded, grad_projected = decoder_pass(
        projected_rows, keep_rows, positions.reshape(-1), upstream, *decoder_args
    )
    grad_compact = jnp.dot(gather, grad_projected, preferred_element_type=jnp.bfloat16)
    mlp_in, grad_pre, hidden, grad_encoded, grad_feats = encode_back(
        saved, grad_compact, enc_params
    )
    device_total = scenes * tiles
    grad_rows = jnp.dot(scatter, grad_feats, preferred_element_type=jnp.bfloat16)
    totals = []
    for left, right in ((mlp_in, grad_pre), (hidden, grad_encoded)):
        term = jnp.dot(left.T, right, preferred_element_type=jnp.float32)
        share = lax.psum_scatter(
            term.astype(jnp.bfloat16), "tile", scatter_dimension=0, tiled=True
        )
        totals.append(lax.psum(share, "dp").astype(jnp.float32))
    fc1_grad, fc2_grad = [total / device_total for total in totals]
    feature_grad = grad_rows.reshape(features.shape)
    decoded_out = decoded.reshape(cotangent.shape)
    return (feature_grad, decoded_out, fc1_grad, fc2_grad)


def solution(mesh):
    return jax.shard_map(
        shards,
        mesh=mesh,
        in_specs=(
            P("dp", "tile", None, None),
            P("dp", "tile", None),
            P("dp", "tile", None),
            P("dp", "tile", None, None),
            P(),
            P(),
            P(),
            P(),
            P(),
            P(),
            P(),
            P(),
            P(),
            P(),
            P(),
            P(),
            P(),
            P(),
        ),
        out_specs=(
            P("dp", "tile", None, None),
            P("dp", "tile", None, None),
            P("tile", None),
            P("tile", None),
        ),
        check_vma=False,
    )
```
